32 devices in a mesh: dp: 4 (over y, core), bucket: 8 (over z, x).
Axes of the slice: x: 2, y: 2, z: 4, core: 2. Of those that a mesh axis runs over, the one named last changes fastest.
Arguments:
- frames: bfloat16 [49152, 512], P(('dp', 'bucket')), may hold values from -60 to 60, as said below
- lengths: int32 [4, 256], P('dp'), may hold values from 1 to 48, as said below
- owners: int32 [4, 256], P('dp'), may hold values from 0 to 7, as said below
- upstream: bfloat16 [24576, 512], P(('dp', 'bucket')), may hold values from -6 to 6
- ln_gain: float32 [512], replicated, may hold values from 0.1 to 1.9
- w_in: bfloat16 [512, 1024], replicated, may hold values from -0.25 to 0.25
- w_dw: float32 [512, 31], replicated, may hold values from -1 to 1
- bn_gain: float32 [512], replicated, may hold values from 0.1 to 1.9
- bn_bias: float32 [512], replicated, may hold values from -3 to 3
- w_out: bfloat16 [512, 512], replicated, may hold values from -0.25 to 0.25
Outputs:
- out_frames: bfloat16 [24576, 512], P(('dp', 'bucket'))
- grad_frames: bfloat16 [49152, 512], P(('dp', 'bucket'))
- grad_w_in: float32 [512, 1024], P('bucket')
- grad_w_out: float32 [512, 512], P('bucket')
- grad_w_dw: float32 [512, 31], P('bucket')
- grad_ln_gain: float32 [512], P('bucket')
- grad_bn_gain: float32 [512], replicated
- grad_bn_bias: float32 [512], replicated
The draws below stay inside these ranges and needn't reach their ends.
Inputs may be any that keep to these rules, and one draw needn't show every extreme that they name: `frames`: frame rows past an utterance's length are not read. In each group every owner receives exactly 4 utterances from each loader shard, their lengths sum to exactly 768 with one of exactly 48, and the lengths an owner receives do not fall with the loader index. `owners`: in each group and loader shard every owner index appears exactly 4 times.
All inputs are finite; a program needn't handle non-finite values.
Results may differ from the reference program's by a relative error of at most 0.013.
Values may be sent and summed in bfloat16 or wider, within the bound.
A program may use at most 128 MiB of HBM per device.

```python
import math
import jax
import jax.numpy as jnp
from jax import lax

D = 512
K = 31
SLOTS = 32
LMAX = 48
GROUPS = 4
LOADERS = 8
PAIR = 4
OWN_ROWS = 768
OWNED_ALL = 24576


def plan_layout(key):
    base_key = jax.random.fold_in(key, 11)
    len_key, perm_key = jax.random.split(base_key)
    cell_count = (SLOTS - 1) * (LMAX - 1)
    deficit = SLOTS * LMAX - OWN_ROWS

    def owner_lengths(sub_key):
        bias_key, noise_key = jax.random.split(sub_key)
        biases = jax.random.randint(bias_key, (SLOTS - 1, 1), 0, 1024)
        noises = jax.random.randint(noise_key, (SLOTS - 1, LMAX - 1), 0, 512)
        scores = ((biases + noises) * cell_count).reshape(-1) + jnp.arange(cell_count, dtype=jnp.int32)
        cell_rank = jnp.argsort(jnp.argsort(scores))
        chosen = (cell_rank < deficit).astype(jnp.int32).reshape(SLOTS - 1, LMAX - 1)
        shorter = LMAX - jnp.sum(chosen, axis=1)
        full_set = jnp.concatenate([jnp.full((1,), LMAX, jnp.int32), shorter.astype(jnp.int32)])
        return jnp.sort(full_set)
    owner_keys = jax.random.split(len_key, GROUPS * LOADERS)
    sorted_lengths = jax.vmap(owner_lengths)(owner_keys).reshape(GROUPS, LOADERS * SLOTS)
    perm_keys = jax.random.split(perm_key, GROUPS * LOADERS)
    entries = jax.vmap(lambda sub_key: jax.random.permutation(sub_key, SLOTS))(perm_keys)
    entries = entries.reshape(GROUPS, LOADERS, SLOTS).astype(jnp.int32)
    owner_of = entries // PAIR
    pair_of = entries % PAIR
    loader_ids = jnp.arange(LOADERS, dtype=jnp.int32)[None, :, None]
    pick_index = (owner_of * SLOTS + loader_ids * PAIR + pair_of).reshape(GROUPS, LOADERS * SLOTS)
    picked = jnp.take_along_axis(sorted_lengths, pick_index, axis=1)
    return (picked.astype(jnp.int32), owner_of.reshape(GROUPS, LOADERS * SLOTS).astype(jnp.int32))


def draw_lengths(key, part):
    return plan_layout(key)[0]


def draw_owners(key, part):
    return plan_layout(key)[1]


def draw_frames(key, part):
    picked, owner_of = plan_layout(key)
    frame_key = jax.random.fold_in(key, 23)
    noise_key, vector_key, row_key = jax.random.split(frame_key, 3)
    row_total = GROUPS * LOADERS * SLOTS * LMAX
    device_rank = jnp.arange(GROUPS, dtype=jnp.int32)[:, None] * LOADERS + owner_of
    ramp_value = device_rank.astype(jnp.float32).reshape(-1) / float(max(GROUPS * LOADERS - 1, 1))
    noise_part = jax.random.normal(noise_key, (row_total, D), jnp.float32)
    row_scale = jnp.exp(jax.random.uniform(row_key, (row_total,), jnp.float32, 0.0, math.log(3.0)))
    amplitude = jnp.exp(ramp_value * math.log(3.0))
    common = jnp.clip(jax.random.normal(vector_key, (D,), jnp.float32), -3.0, 3.0)
    strength = 0.25 * jnp.repeat(amplitude, LMAX) * row_scale
    return (noise_part + strength[:, None] * common[None, :]).astype(jnp.bfloat16)


def levels(own_key, dims, cuts, least, high):
    gain, own = 1.0, jax.random.fold_in(own_key, 6)
    for axis_at, shards_of in cuts:
        heights = jnp.exp(jax.random.uniform(jax.random.fold_in(own, axis_at), (shards_of,), jnp.float32, least / len(cuts), high / len(cuts)))
        gain = gain * jnp.repeat(heights, dims[axis_at] // shards_of).reshape([-1 if axis == axis_at else 1 for axis in range(len(dims))])
    return gain


def noise(own_key, extent, deviation, most, shards=(), kind=jnp.bfloat16):
    values = jax.random.normal(own_key, extent, jnp.float32) * deviation
    if len(shards) > 0:
        values = levels(own_key, extent, shards, -0.22, 0.18) * values
    return jnp.clip(values, min=-most, max=most).astype(kind)


def setup_inputs(seed: int = 0) -> dict:
    seeds = jax.random.split(jax.random.key(seed), 11)
    return {
        "frames": draw_frames(jax.random.fold_in(seeds[10], 71), 0),
        "lengths": draw_lengths(jax.random.fold_in(seeds[10], 71), 0),
        "owners": draw_owners(jax.random.fold_in(seeds[10], 71), 0),
        "upstream": noise(seeds[3], (OWNED_ALL, D), 1.0, 6.0, ((0, 32),)),
        "ln_gain": jnp.clip(1.0 + 0.18 * jax.random.normal(seeds[4], (D,), jnp.float32), 0.1, 1.9),
        "w_in": noise(seeds[5], (D, 2 * D), D ** -0.5, 0.25),
        "w_dw": noise(seeds[6], (D, K), K ** -0.5, 1.0, (), jnp.float32),
        "bn_gain": jnp.clip(1.0 + 0.18 * jax.random.normal(seeds[7], (D,), jnp.float32), 0.1, 1.9),
        "bn_bias": noise(seeds[8], (D,), 0.5, 3.0, (), jnp.float32),
        "w_out": noise(seeds[9], (D, D), D ** -0.5, 0.25),
    }


EPSILON = 1e-05

def normalize_rows(frame_rows, ln_gain):
    values = frame_rows.astype(jnp.float32)
    centred = values - lax.optimization_barrier(jnp.mean(values, axis=1, keepdims=True))
    inverse = lax.rsqrt(lax.optimization_barrier(jnp.mean(centred * centred, axis=1, keepdims=True)) + EPSILON)
    normed = centred * inverse
    return ((normed * ln_gain).astype(jnp.bfloat16), normed, inverse)

def normalize_back(grad_h, normed, inverse, ln_gain):
    scaled = grad_h * ln_gain
    inner_sum = lax.optimization_barrier(jnp.mean(scaled * normed, axis=1, keepdims=True))
    return inverse * (scaled - lax.optimization_barrier(jnp.mean(scaled, axis=1, keepdims=True)) - normed * inner_sum)

def conv_forward(gated_rows, segment, w_dw):
    width_half = w_dw.shape[1] // 2
    length_all = gated_rows.shape[1]
    padded = jnp.pad(gated_rows, ((0, 0), (width_half, width_half), (0, 0)))
    seg_pad = jnp.pad(segment, ((0, 0), (width_half, width_half)), constant_values=-1)
    result = jnp.zeros(gated_rows.shape, jnp.float32)
    for offset in range(w_dw.shape[1]):
        same_seg = (seg_pad[:, offset:offset + length_all] == segment)[:, :, None]
        shifted = padded[:, offset:offset + length_all].astype(jnp.float32)
        result = result + jnp.where(same_seg, shifted, 0.0) * w_dw[:, offset]
    return result

def conv_backward(grad_conv, gated_rows, segment, w_dw):
    width_half = w_dw.shape[1] // 2
    length_all = gated_rows.shape[1]
    padded = jnp.pad(gated_rows, ((0, 0), (width_half, width_half), (0, 0)))
    grad_pad = jnp.pad(grad_conv, ((0, 0), (width_half, width_half), (0, 0)))
    seg_pad = jnp.pad(segment, ((0, 0), (width_half, width_half)), constant_values=-1)
    grad_gated = jnp.zeros(grad_conv.shape, jnp.float32)
    grad_cols = []
    for offset in range(w_dw.shape[1]):
        same_fwd = (seg_pad[:, offset:offset + length_all] == segment)[:, :, None]
        shifted = jnp.where(same_fwd, padded[:, offset:offset + length_all].astype(jnp.float32), 0.0)
        grad_cols.append(lax.optimization_barrier(jnp.sum(shifted * grad_conv, axis=(0, 1))))
        back_start = 2 * width_half - offset
        same_back = (seg_pad[:, back_start:back_start + length_all] == segment)[:, :, None]
        grad_gated = grad_gated + jnp.where(same_back, grad_pad[:, back_start:back_start + length_all], 0.0) * w_dw[:, offset]
    return (grad_gated, jnp.stack(grad_cols, axis=1))

def reference(frames, lengths, owners, upstream, ln_gain, w_in, w_dw, bn_gain, bn_bias, w_out):
    utterances = LOADERS * SLOTS
    frame_groups = frames.reshape(GROUPS, utterances * LMAX, D)
    grad_groups = upstream.reshape(GROUPS, LOADERS * OWN_ROWS, D)
    position = jnp.arange(LMAX, dtype=jnp.int32)
    segment = jnp.broadcast_to(jnp.arange(utterances, dtype=jnp.int32)[:, None], (utterances, LMAX))
    total_frames = float(GROUPS * LOADERS * OWN_ROWS)
    owner_ids = jnp.arange(LOADERS, dtype=jnp.int32)

    def layout(lens_group, dest_group):
        valid_rows = position[None, :] < lens_group[:, None]
        onehot = (dest_group[:, None] == owner_ids[None, :]).astype(jnp.int32)
        weighted = onehot * lens_group[:, None]
        earlier = jnp.cumsum(weighted, axis=0) - weighted
        starts = lax.optimization_barrier(jnp.sum(earlier * onehot, axis=1))
        target = dest_group[:, None] * OWN_ROWS + starts[:, None] + position[None, :]
        target = jnp.where(valid_rows, target, LOADERS * OWN_ROWS)
        return target.reshape(-1).astype(jnp.int32)

    def forward(frame_block, lens_group):
        valid_rows = (position[None, :] < lens_group[:, None]).reshape(-1)
        normed_h, normed, inverse = normalize_rows(frame_block, ln_gain)
        projected = jnp.dot(normed_h, w_in, preferred_element_type=jnp.float32)
        linear = projected[:, :D]
        gate_sig = jax.nn.sigmoid(projected[:, D:])
        gated_rows = jnp.where(valid_rows[:, None], linear * gate_sig, 0.0).astype(jnp.bfloat16)
        conv_rows = conv_forward(gated_rows.reshape(utterances, LMAX, D), segment, w_dw).reshape(-1, D)
        return (valid_rows, normed_h, normed, inverse, linear, gate_sig, gated_rows, conv_rows)

    def moments(inputs_group):
        frame_block, lens_group = inputs_group
        valid_rows = forward(frame_block, lens_group)[0]
        conv_rows = forward(frame_block, lens_group)[7]
        masked = jnp.where(valid_rows[:, None], conv_rows, 0.0)
        return (lax.optimization_barrier(jnp.sum(masked, axis=0)), lax.optimization_barrier(jnp.sum(masked * masked, axis=0)))
    first_parts, second_parts = lax.map(moments, (frame_groups, lengths))
    centre = lax.optimization_barrier(jnp.sum(first_parts, axis=0)) / total_frames
    variance = lax.optimization_barrier(jnp.sum(second_parts, axis=0)) / total_frames - centre * centre
    bn_inverse = lax.rsqrt(variance + EPSILON)

    def batch_part(conv_rows):
        bn_normed = (conv_rows - centre) * bn_inverse
        bn_value = bn_normed * bn_gain + bn_bias
        bn_sig = jax.nn.sigmoid(bn_value)
        swished = (bn_value * bn_sig).astype(jnp.bfloat16)
        return (bn_normed, bn_value, bn_sig, swished)

    def grad_slots(grad_block, valid_rows, target):
        picked = jnp.take(grad_block, jnp.minimum(target, LOADERS * OWN_ROWS - 1), axis=0)
        return jnp.where(valid_rows[:, None], picked, 0.0).astype(jnp.bfloat16)

    def second_pass(inputs_group):
        frame_block, grad_block, lens_group, dest_group = inputs_group
        target = layout(lens_group, dest_group)
        valid_rows, normed_h, normed, inverse, linear, gate_sig, gated_rows, conv_rows = forward(frame_block, lens_group)
        bn_normed, bn_value, bn_sig, swished = batch_part(conv_rows)
        out_rows = jnp.dot(swished, w_out, preferred_element_type=jnp.float32).astype(jnp.bfloat16)
        packed = jnp.zeros((LOADERS * OWN_ROWS, D), jnp.bfloat16).at[target].set(out_rows, mode='drop')
        grad_out = grad_slots(grad_block, valid_rows, target)
        grad_swish = jnp.dot(grad_out, w_out.T, preferred_element_type=jnp.float32)
        grad_bn_rows = grad_swish * (bn_sig * (1.0 + bn_value * (1.0 - bn_sig)))
        return (packed, lax.optimization_barrier(jnp.sum(grad_bn_rows, axis=0)), lax.optimization_barrier(jnp.sum(grad_bn_rows * bn_normed, axis=0)))
    packed_all, bias_parts, gain_parts = lax.map(second_pass, (frame_groups, grad_groups, lengths, owners))
    bias_total = lax.optimization_barrier(jnp.sum(bias_parts, axis=0))
    gain_total = lax.optimization_barrier(jnp.sum(gain_parts, axis=0))

    def third_pass(inputs_group):
        frame_block, grad_block, lens_group, dest_group = inputs_group
        target = layout(lens_group, dest_group)
        valid_rows, normed_h, normed, inverse, linear, gate_sig, gated_rows, conv_rows = forward(frame_block, lens_group)
        bn_normed, bn_value, bn_sig, swished = batch_part(conv_rows)
        grad_out = grad_slots(grad_block, valid_rows, target)
        grad_wout = jnp.dot(swished.T, grad_out, preferred_element_type=jnp.float32)
        grad_swish = jnp.dot(grad_out, w_out.T, preferred_element_type=jnp.float32)
        grad_bn_rows = grad_swish * (bn_sig * (1.0 + bn_value * (1.0 - bn_sig)))
        grad_conv = jnp.where(valid_rows[:, None], bn_gain * bn_inverse * (grad_bn_rows - bias_total / total_frames - bn_normed * (gain_total / total_frames)), 0.0)
        grad_gated, grad_wdw = conv_backward(grad_conv.reshape(utterances, LMAX, D), gated_rows.reshape(utterances, LMAX, D), segment, w_dw)
        grad_gated = jnp.where(valid_rows[:, None], grad_gated.reshape(-1, D), 0.0)
        grad_proj = jnp.concatenate([grad_gated * gate_sig, grad_gated * linear * gate_sig * (1.0 - gate_sig)], axis=1).astype(jnp.bfloat16)
        grad_win = jnp.dot(normed_h.T, grad_proj, preferred_element_type=jnp.float32)
        grad_h = jnp.dot(grad_proj, w_in.T, preferred_element_type=jnp.float32)
        grad_ln = lax.optimization_barrier(jnp.sum(grad_h * normed, axis=0))
        grad_rows = normalize_back(grad_h, normed, inverse, ln_gain)
        grad_rows = jnp.where(valid_rows[:, None], grad_rows, 0.0).astype(jnp.bfloat16)
        return (grad_rows, grad_win, grad_wout, grad_wdw, grad_ln)
    grad_all, win_parts, wout_parts, wdw_parts, ln_parts = lax.map(third_pass, (frame_groups, grad_groups, lengths, owners))
    return (packed_all.reshape(-1, D), grad_all.reshape(-1, D), lax.optimization_barrier(jnp.sum(win_parts, axis=0)), lax.optimization_barrier(jnp.sum(wout_parts, axis=0)), lax.optimization_barrier(jnp.sum(wdw_parts, axis=0)), lax.optimization_barrier(jnp.sum(ln_parts, axis=0)), gain_total, bias_total)
```

```python
import functools

import jax
import jax.numpy as jnp
import numpy as np
from jax import lax
from jax.experimental import pallas as pl
from jax.experimental.pallas import tpu as pltpu
from jax.sharding import PartitionSpec as P

EPSILON = 1e-05
LANES = 128
SUB = 8
PACK = 16
MESH = pl.DeviceIdType.MESH
BF16 = jnp.bfloat16
F32 = jnp.float32


def lane(c):
    return slice(c * LANES, (c + 1) * LANES)


def row_of(packed, first, blocks):
    return jnp.concatenate([packed[first + c : first + c + 1] for c in range(blocks)], axis=1)


def keep_live(values, lengths, span):
    position = lax.broadcasted_iota(jnp.int32, (span, values.shape[1]), 0)
    parts = [
        jnp.where(position < length, values[i * span : (i + 1) * span], 0.0)
        for i, length in enumerate(lengths)
    ]
    return jnp.concatenate(parts, axis=0)


def fold_rows(values):
    rows, width = values.shape
    return jnp.sum(values.reshape(rows // SUB, SUB, width), axis=0)


def matmul(a, b):
    return jnp.dot(a, b, preferred_element_type=F32)


def matmul_nt(a, b):
    return lax.dot_general(a, b, (((1,), (1,)), ((), ())), preferred_element_type=F32)


def matmul_tn(a, b):
    return lax.dot_general(a, b, (((0,), (0,)), ((), ())), preferred_element_type=F32)


def matmul_exact(a, b):
    return jnp.dot(a, b, preferred_element_type=F32, precision=lax.Precision.HIGHEST)


def transform_tables(span, taps, group):
    size = -(-(span + taps // 2) // (2 * PACK)) * (2 * PACK)
    half = size // 2
    freq = np.arange(half)[:, None]

    def angle(times):
        return 2.0 * np.pi * freq * np.asarray(times)[None, :] / size

    def flip(times):
        return np.where(np.asarray(times) % 2 == 0, 1.0, -1.0)

    times = np.arange(span)
    real, imag = np.cos(angle(times)), -np.sin(angle(times))
    imag[0] = flip(times)
    forward = np.concatenate([real, imag], axis=0)
    scale = np.where(np.arange(size) % half == 0, 1.0, 2.0) / size
    inverse = (forward * scale[:, None]).T
    lags = taps // 2 - np.arange(taps)
    wr, wi, wn = np.cos(angle(lags)), -np.sin(angle(lags)), np.cos(angle(lags))
    wi[0] = 0.0
    wn[0] = flip(lags)
    spectrum = np.concatenate([wr, wi, wn], axis=0)
    spectrum = np.pad(spectrum, ((0, 0), (0, 1)))
    back = -lags
    cr, cn, ci = np.cos(angle(back)), np.cos(angle(back)), -np.sin(angle(back))
    cn[0] = flip(back)
    ci[0] = 0.0
    both = np.concatenate([scale[:half], scale[half:], scale[half:]])
    correlate = (np.concatenate([cr, cn, ci], axis=0) * both[:, None]).T
    correlate = np.pad(correlate, ((0, 1), (0, 0)))
    eye = np.eye(group)
    return (
        size,
        jnp.asarray(np.kron(eye, forward), BF16),
        jnp.asarray(np.kron(eye, inverse), BF16),
        jnp.asarray(spectrum, F32),
        jnp.asarray(correlate, F32),
    )


def tables_kernel(slots, lens_ref, owners_ref, meta_ref, counts):
    me = lax.axis_index("bucket")
    loaders = lens_ref.shape[1] // slots
    pairs = slots // loaders

    def look(i, carry):
        found, start = carry
        for j in range(SUB):
            at = i * SUB + j
            mine = owners_ref[0, at] == me
            meta_ref[2, found] = start
            found = found + jnp.where(mine, 1, 0)
            start = start + jnp.where(mine, lens_ref[0, at], 0)
        return found, start

    lax.fori_loop(0, loaders * slots // SUB, look, (jnp.int32(0), jnp.int32(0)))

    def clear(i, carry):
        counts[i] = 0
        return carry

    lax.fori_loop(0, loaders, clear, 0)

    def place(i, carry):
        owner = owners_ref[0, me * slots + i]
        rank = counts[owner]
        counts[owner] = rank + 1
        at = owner * pairs + rank
        meta_ref[0, at] = lens_ref[0, me * slots + i]
        meta_ref[1, at] = i
        return carry

    lax.fori_loop(0, slots, place, 0)


def step_kernel(
    groups, owners, group, taps, size, early, total_frames,
    meta, frames_hbm, up_hbm, w_in_hbm, w_out_hbm, gain_ref, bn_gain_ref, bn_bias_ref, w_taps_ref,
    fwd_ref, inv_ref, spec_ref, corr_ref,
    grads_ref, arrived_ref, reduced_ref, back_ref, ln_ref,
    frames, up, w_in_ref, w_out_ref, stage, outgoing, arrive, outbuf,
    normed_s, inverse_s, linear_s, gate_s, h_s, spect_s, conv_s, fac_s, sw_s, dy_s, ga_s,
    wspec, acc, xacc, tot, parts, slots_s, flat,
    packed, first, first_sum, second, second_sum, third, mine,
    local_sems, sum_send, sum_recv, up_send, up_recv, out_send, out_recv,
    core_sems, pair_sems, row_sems, all_sems,
):
    dp, me = lax.axis_index("dp"), lax.axis_index("bucket")
    slot_count, span, width = frames.shape
    all_rows = slot_count * span
    own_rows = up.shape[0]
    blocks = width // LANES
    wide = w_in_ref.shape[1] // LANES
    chunk = all_rows // owners
    pairs = slot_count // owners
    steps = slot_count // group
    held = group // pairs
    grows = group * span
    half = size // 2
    count = groups * owners
    rank = dp * owners + me
    barrier = pltpu.get_barrier_semaphore()

    def device_of(i):
        other = lax.rem(rank + i, count)
        return (other // owners, lax.rem(other, owners))

    def greet(i, carry):
        pl.semaphore_signal(barrier, inc=1, device_id=device_of(i), device_id_type=MESH)
        return carry

    lax.fori_loop(1, count, greet, 0)
    loads = [
        pltpu.make_async_copy(source, target, local_sems.at[n])
        for n, (source, target) in enumerate(
            ((up_hbm, up), (frames_hbm, frames), (w_in_hbm, w_in_ref), (w_out_hbm, w_out_ref))
        )
    ]
    for load in loads:
        load.start()

    loads[0].wait()
    for c in range(blocks):
        stage[c, :own_rows] = up[:, lane(c)].astype(F32)
        stage[c, own_rows:] = jnp.zeros((span, LANES), F32)

    def lay_out(b, carry):
        for q in range(pairs):
            start = meta[2, b * pairs + q]
            for c in range(blocks):
                outgoing[b, q * span : (q + 1) * span, lane(c)] = stage[
                    c, pl.ds(start, span)
                ].astype(BF16)
        return carry

    lax.fori_loop(0, owners, lay_out, 0)
    arrive[me] = outgoing[me]

    def offset_of(j):
        return lax.rem(owners // 2 + j, owners) + (j // (owners - owners // 2))

    def up_copy(j, part, arriving):
        offset = offset_of(j)
        target = lax.rem(me + offset, owners)
        slot = lax.rem(me + owners - offset, owners) if arriving else me
        rows = pl.ds(0, early) if part == 0 else pl.ds(early, chunk - early)
        return pltpu.make_async_remote_copy(
            src_ref=outgoing.at[target, rows],
            dst_ref=arrive.at[slot, rows],
            send_sem=up_send.at[part, j],
            recv_sem=up_recv.at[part, j],
            device_id=(dp, target),
            device_id_type=MESH,
        )

    def start_up(part):
        def body(j, carry):
            up_copy(j, part, False).start()
            return carry

        lax.fori_loop(0, owners - 1, body, 0)

    def out_copy(j, arriving):
        offset = offset_of(j)
        target = lax.rem(me + offset, owners)
        slot = lax.rem(me + owners - offset, owners) if arriving else me
        return pltpu.make_async_remote_copy(
            src_ref=outbuf.at[target],
            dst_ref=arrived_ref.at[slot],
            send_sem=out_send.at[j],
            recv_sem=out_recv.at[j],
            device_id=(dp, target),
            device_id_type=MESH,
        )

    def sum_copy(n, i, slot):
        return pltpu.make_async_remote_copy(
            src_ref=parts.at[n],
            dst_ref=slots_s.at[n, slot],
            send_sem=sum_send.at[n, i],
            recv_sem=sum_recv.at[n, slot],
            device_id=device_of(i),
            device_id_type=MESH,
        )

    def sum_start(n):
        def send(i, carry):
            sum_copy(n, i, rank).start()
            return carry

        lax.fori_loop(1, count, send, 0)
        slots_s[n, rank] = parts[n]

    def sum_finish(n):
        def receive(i, carry):
            sum_copy(n, i, lax.rem(rank + i, count)).wait_recv()
            return carry

        lax.fori_loop(1, count, receive, 0)
        return lax.fori_loop(
            1, count, lambda i, total: total + slots_s[n, i], slots_s[n, 0]
        )

    def gather_parts(n):
        for k in range(2):
            row = jnp.sum(acc[k], axis=0, keepdims=True)
            for c in range(blocks):
                parts[n, k * blocks + c : k * blocks + c + 1] = row[:, lane(c)]

    wspec[...] = matmul_exact(spec_ref[...], w_taps_ref[...])
    acc[...] = jnp.zeros_like(acc)
    pl.semaphore_wait(barrier, count - 1)
    start_up(0)
    loads[1].wait()
    loads[2].wait()

    def rows_of(i):
        return pl.ds(pl.multiple_of(i * grows, PACK), grows)

    def spec_rows(i):
        return pl.ds(pl.multiple_of(i * group * size, PACK), group * size)

    def lengths_of(i):
        return [meta[0, i * group + u] for u in range(group)]

    def forward(i, carry):
        rows = rows_of(i)
        lengths = lengths_of(i)
        values = jnp.concatenate(
            [frames[meta[1, i * group + u]] for u in range(group)], axis=0
        ).astype(F32)
        centred = values - jnp.mean(values, axis=1, keepdims=True)
        inverse = lax.rsqrt(jnp.mean(centred * centred, axis=1, keepdims=True) + EPSILON)
        normed = centred * inverse
        h = (normed * gain_ref[...]).astype(BF16)
        projected = matmul(h, w_in_ref[...])
        linear, gate = projected[:, :width], jax.nn.sigmoid(projected[:, width:])
        normed_s[rows] = normed
        inverse_s[rows] = jnp.broadcast_to(inverse, (grows, LANES))
        linear_s[rows] = linear
        gate_s[rows] = gate
        h_s[rows] = h
        gated = keep_live(linear * gate, lengths, span).astype(BF16)
        spect = matmul(fwd_ref[...], gated)
        spect_s[spec_rows(i)] = spect
        wr, wi, wn = wspec[:half], wspec[half : 2 * half], wspec[2 * half :]
        mixed = []
        for u in range(group):
            re = spect[u * size : u * size + half]
            im = spect[u * size + half : (u + 1) * size]
            mixed.append((wr * re - wi * im).astype(BF16))
            mixed.append((wn * im + wi * re).astype(BF16))
        conv = matmul(inv_ref[...], jnp.concatenate(mixed, axis=0))
        conv_s[rows] = conv
        masked = keep_live(conv, lengths, span)
        acc[0] += fold_rows(masked)
        acc[1] += fold_rows(masked * masked)
        return carry

    lax.fori_loop(0, steps, forward, 0)
    gather_parts(0)
    sum_start(0)
    start_up(1)
    loads[3].wait()
    tot[...] = sum_finish(0)
    centre = row_of(tot, 0, blocks) / total_frames
    variance = row_of(tot, blocks, blocks) / total_frames - centre * centre
    bn_inverse = lax.rsqrt(variance + EPSILON)
    acc[...] = jnp.zeros_like(acc)
    bn_gain, bn_bias = bn_gain_ref[...], bn_bias_ref[...]

    def swish(i, carry):
        rows = rows_of(i)
        bn_normed = (conv_s[rows] - centre) * bn_inverse
        conv_s[rows] = bn_normed
        bn = bn_normed * bn_gain + bn_bias
        sig = jax.nn.sigmoid(bn)
        swished = (bn * sig).astype(BF16)
        sw_s[rows] = swished
        fac_s[rows] = sig * (1.0 + bn * (1.0 - sig))
        out = matmul(swished, w_out_ref[...]).astype(BF16)
        for r in range(held):
            outbuf[i * held + r] = out[r * chunk : (r + 1) * chunk]
        return carry

    lax.fori_loop(0, steps, swish, 0)
    my_step = me // held

    def middle(t, carry):
        late = lax.rem(t + steps - 1, steps)
        offset = lax.rem(steps // 2 + late, steps) + (late // (steps - steps // 2))
        i = lax.rem(my_step + 2 * steps - offset * ((t + steps - 1) // steps), steps)
        rows = rows_of(i)
        lengths = lengths_of(i)
        for r in range(held):
            owner = i * held + r

            @pl.when(owner != me)
            def _():
                gap = lax.rem(me + owners - owner, owners)
                j = lax.rem(gap + owners - owners // 2, owners) - (
                    (owners // 2 - 1 + owners - gap) // owners
                )
                up_copy(j, 0, True).wait_recv()
                up_copy(j, 1, True).wait_recv()

        arrived = jnp.concatenate([arrive[i * held + r] for r in range(held)], axis=0)
        dy = keep_live(arrived.astype(F32), lengths, span).astype(BF16)
        dy_s[rows] = dy
        grad_bn = matmul_nt(dy, w_out_ref[...]) * fac_s[rows]
        fac_s[rows] = grad_bn
        acc[0] += fold_rows(grad_bn)
        acc[1] += fold_rows(grad_bn * conv_s[rows])
        return carry

    lax.fori_loop(0, steps, middle, 0)
    gather_parts(1)
    sum_start(1)

    def start_out(j, carry):
        out_copy(j, False).start()
        return carry

    lax.fori_loop(0, owners - 1, start_out, 0)
    arrived_ref[me] = outbuf[me]

    chunk_rows = packed.shape[3]
    share = width // owners
    sections = wide + blocks
    per = -(-sections // groups)
    piece = share // groups
    sides = groups // 2

    def put(j, section, block):
        q, r = section // per, section % per
        packed[j, q // sides, q % sides, r * share : (r + 1) * share] = block.astype(BF16)

    if per * groups != sections or chunk_rows != per * share + piece:
        packed[...] = jnp.zeros_like(packed)
    for c in range(blocks):
        grad = matmul_tn(sw_s[:, lane(c)], dy_s[...])
        for n in range(LANES // share):
            for s in range(blocks):
                put(c * (LANES // share) + n, wide + s, grad[n * share : (n + 1) * share, lane(s)])

    back_ref[...] = sum_finish(1)
    bias_mean = row_of(back_ref, 0, blocks) / total_frames
    gain_mean = row_of(back_ref, blocks, blocks) / total_frames
    scale = bn_gain * bn_inverse
    xacc[...] = jnp.zeros_like(xacc)

    def backward(i, carry):
        rows = rows_of(i)
        lengths = lengths_of(i)
        grad_conv = scale * (fac_s[rows] - bias_mean - conv_s[rows] * gain_mean)
        grad_conv = keep_live(grad_conv, lengths, span).astype(BF16)
        spect = matmul(fwd_ref[...], grad_conv)
        saved = spect_s[spec_rows(i)]
        wr, wi, wn = wspec[:half], wspec[half : 2 * half], wspec[2 * half :]
        mixed, terms = [], [None] * 3
        for u in range(group):
            re = spect[u * size : u * size + half]
            im = spect[u * size + half : (u + 1) * size]
            sre = saved[u * size : u * size + half]
            sim = saved[u * size + half : (u + 1) * size]
            mixed.append((wr * re + wi * im).astype(BF16))
            mixed.append((wn * im - wi * re).astype(BF16))
            new = (re * sre, im * sim, re * sim - im * sre)
            terms = [b if a is None else a + b for a, b in zip(terms, new)]
        for n in range(3):
            xacc[n * half : (n + 1) * half] += terms[n]
        grad_gated = matmul(inv_ref[...], jnp.concatenate(mixed, axis=0))
        grad_gated = keep_live(grad_gated, lengths, span)
        gate = gate_s[rows]
        left = grad_gated * gate
        ga_s[rows, :width] = left.astype(BF16)
        ga_s[rows, width:] = (left * linear_s[rows] * (1.0 - gate)).astype(BF16)
        return carry

    lax.fori_loop(0, steps, backward, 0)
    grad_taps = matmul_exact(corr_ref[...], xacc[...])
    flat[...] = jnp.zeros_like(flat)
    for c in range(blocks):
        grad = matmul_tn(h_s[:, lane(c)], ga_s[...])
        flat[: taps + 1] = grad_taps[:, lane(c)]
        turned = flat[...].T.astype(BF16)
        for n in range(LANES // share):
            j = c * (LANES // share) + n
            for s in range(wide):
                put(j, s, grad[n * share : (n + 1) * share, lane(s)])
            for q in range(groups):
                packed[j, q // sides, q % sides, per * share : per * share + piece] = turned[
                    n * share + q * piece : n * share + (q + 1) * piece
                ]

    core, side = lax.rem(dp, 2), dp // 2
    partner = side * 2 + (1 - core)

    def remote(source, target, sems, i, j, device):
        return pltpu.make_async_remote_copy(
            src_ref=source,
            dst_ref=target,
            send_sem=sems.at[0, i],
            recv_sem=sems.at[1, j],
            device_id=device,
            device_id_type=MESH,
        )

    def bucket_of(i):
        return lax.rem(me + 1 + i, owners)

    def swap(i):
        bucket = bucket_of(i)
        return remote(packed.at[bucket, 1 - core], first.at[bucket], core_sems, i, i, (partner, me))

    def to_side(i, n, arriving):
        bucket = bucket_of(i)
        other = lax.rem(side + n, sides)
        slot = other if arriving else side
        return remote(
            first_sum.at[bucket, other], second.at[slot, bucket], pair_sems,
            n * owners + i, slot * owners + i, (other * 2 + core, me),
        )

    def to_owner(i, arriving):
        other = lax.rem(me + i, owners)
        slot = other if arriving else me
        return remote(second_sum.at[other], third.at[slot], row_sems, i, slot, (dp, other))

    def to_group(i, arriving):
        other = lax.rem(dp + i, groups)
        device = other if arriving else dp
        slot = lax.rem(device, 2) * sides + device // 2
        return remote(mine, reduced_ref.at[slot], all_sems, i, slot, (other, me))

    def start_swap(i, carry):
        swap(i).start()
        return carry

    def add_first(i, carry):
        bucket = bucket_of(i)
        swap(i).wait_recv()
        total = packed[bucket, core].astype(F32) + first[bucket].astype(F32)
        first_sum[bucket] = total.astype(BF16)
        for n in range(1, sides):
            to_side(i, n, False).start()
        return carry

    def add_second(i, carry):
        bucket = bucket_of(i)
        total = first_sum[bucket, side].astype(F32)
        for n in range(1, sides):
            to_side(i, n, True).wait_recv()
            total = total + second[lax.rem(side + n, sides), bucket].astype(F32)
        second_sum[bucket] = total.astype(BF16)
        return carry

    def add_and_send(i, carry):
        add_second(i, carry)
        to_owner(i + 1, False).start()
        return carry

    lax.fori_loop(0, owners, start_swap, 0)
    acc[...] = jnp.zeros_like(acc)

    def last(i, carry):
        rows = rows_of(i)
        lengths = lengths_of(i)
        grad_h = matmul_nt(ga_s[rows], w_in_ref[...])
        normed, inverse = normed_s[rows], inverse_s[rows][:, :1]
        acc[0] += fold_rows(grad_h * normed)
        scaled = grad_h * gain_ref[...]
        inner_mean = jnp.mean(scaled * normed, axis=1, keepdims=True)
        grad_x = inverse * (scaled - jnp.mean(scaled, axis=1, keepdims=True) - normed * inner_mean)
        grads_ref[rows] = keep_live(grad_x, lengths, span).astype(BF16)
        return carry

    lax.fori_loop(0, steps // 4, last, 0)
    lax.fori_loop(0, owners, add_first, 0)
    lax.fori_loop(steps // 4, steps // 2, last, 0)
    lax.fori_loop(0, owners - 1, add_and_send, 0)
    add_second(owners - 1, 0)
    third[me] = second_sum[me]
    lax.fori_loop(steps // 2, steps, last, 0)
    gather_parts(2)
    sum_start(2)

    def wait_owner(i, carry):
        to_owner(i, True).wait_recv()
        return carry

    lax.fori_loop(1, owners, wait_owner, 0)
    total = lax.fori_loop(
        1, owners, lambda i, t: t + third[i].astype(F32), third[0].astype(F32)
    )
    mine[...] = total.astype(BF16)

    def send_group(i, carry):
        to_group(i, False).start()
        return carry

    def wait_group(i, carry):
        to_group(i, True).wait_recv()
        return carry

    lax.fori_loop(1, groups, send_group, 0)
    reduced_ref[core * sides + side] = mine[...]
    ln_ref[...] = sum_finish(2)
    lax.fori_loop(1, groups, wait_group, 0)

    def finish_out(j, carry):
        out_copy(j, True).wait_recv()
        out_copy(j, False).wait_send()
        up_copy(j, 0, False).wait_send()
        up_copy(j, 1, False).wait_send()
        return carry

    lax.fori_loop(0, owners - 1, finish_out, 0)

    def finish_sums(i, carry):
        for n in range(3):
            sum_copy(n, i, rank).wait_send()
        return carry

    lax.fori_loop(1, count, finish_sums, 0)

    def finish_first(i, carry):
        swap(i).wait_send()
        for n in range(1, sides):
            to_side(i, n, False).wait_send()
        return carry

    def finish_owner(i, carry):
        to_owner(i, False).wait_send()
        return carry

    def finish_group(i, carry):
        to_group(i, False).wait_send()
        return carry

    lax.fori_loop(0, owners, finish_first, 0)
    lax.fori_loop(1, owners, finish_owner, 0)
    lax.fori_loop(1, groups, finish_group, 0)


def finish_kernel(
    taps, per, piece,
    meta, grads_ref, arrived_ref, reduced_ref, back_ref, ln_ref,
    out_ref, grad_frames_ref, win_ref, wout_ref, taps_ref, ln_out_ref, gain_ref, bias_ref,
    stage, flat, sems,
):
    me = lax.axis_index("bucket")
    slots, span, width = arrived_ref.shape
    own_rows = out_ref.shape[0]
    blocks = width // LANES
    share = win_ref.shape[0]
    wide = win_ref.shape[1] // LANES
    owners = width // share

    def row_copy(i):
        source = pl.ds(pl.multiple_of(i * span, PACK), span)
        target = pl.ds(pl.multiple_of(meta[1, i] * span, PACK), span)
        return pltpu.make_async_copy(
            grads_ref.at[source], grad_frames_ref.at[target], sems.at[i]
        )

    def start(i, carry):
        row_copy(i).start()
        return carry

    lax.fori_loop(0, slots, start, 0)

    def place(u, carry):
        begin = meta[2, u]
        for c in range(blocks):
            stage[c, pl.ds(begin, span)] = arrived_ref[u, :, lane(c)].astype(F32)
        return carry

    lax.fori_loop(0, slots, place, 0)

    def section(s):
        q, r = s // per, s % per
        return reduced_ref[q, r * share : (r + 1) * share].astype(F32)

    for c in range(blocks):
        out_ref[:, lane(c)] = stage[c, :own_rows].astype(BF16)
        wout_ref[:, lane(c)] = section(wide + c)
    for c in range(wide):
        win_ref[:, lane(c)] = section(c)
    flat[...] = jnp.zeros_like(flat)
    for q in range(reduced_ref.shape[0]):
        flat[q * piece : (q + 1) * piece] = reduced_ref[
            q, per * share : per * share + piece
        ].astype(F32)
    taps_ref[...] = flat[...].T[:taps, :share]
    row = jnp.zeros((1, share), F32)
    for j in range(owners):
        c, n = j * share // LANES, j * share % LANES
        row = jnp.where(me == j, ln_ref[c : c + 1, n : n + share], row)
    ln_out_ref[...] = row
    bias_ref[...] = row_of(back_ref, 0, blocks)
    gain_ref[...] = row_of(back_ref, blocks, blocks)

    def wait(i, carry):
        row_copy(i).wait()
        return carry

    lax.fori_loop(0, slots, wait, 0)


def in_hbm(array):
    return pltpu.with_memory_space_constraint(array, pltpu.HBM)


def local(frames, lengths, owner_ids, upstream, ln_gain, w_in, w_dw, bn_gain, bn_bias, w_out):
    groups, owners = lax.axis_size("dp"), lax.axis_size("bucket")
    all_rows, width = frames.shape
    taps = w_dw.shape[1]
    slots = lengths.shape[1] // owners
    span = all_rows // slots
    pairs = slots // owners
    own_rows = upstream.shape[0]
    blocks = width // LANES
    wide = w_in.shape[1] // LANES
    count = groups * owners
    total_frames = float(own_rows * count)
    in_vmem = pl.BlockSpec(memory_space=pltpu.VMEM)
    in_smem = pl.BlockSpec(memory_space=pltpu.SMEM)
    anywhere = pl.BlockSpec(memory_space=pl.ANY)
    group = pairs * max(1, 4 // pairs)
    size, fwd, inv, spec, corr = transform_tables(span, taps, group)
    chunk = pairs * span
    early = -(-chunk // 3 // PACK) * PACK
    share = width // owners
    per = -(-(wide + blocks) // groups)
    piece = share // groups
    chunk_rows = per * share + -(-piece // PACK) * PACK
    sides = groups // 2

    meta = pl.pallas_call(
        functools.partial(tables_kernel, slots),
        in_specs=[in_smem, in_smem],
        out_specs=in_smem,
        out_shape=jax.ShapeDtypeStruct((3, slots + SUB), jnp.int32),
        scratch_shapes=[pltpu.SMEM((owners,), jnp.int32)],
        name="tables",
    )(in_hbm(lengths), in_hbm(owner_ids))

    sums_shape = (2 * blocks, LANES)
    tall = pltpu.VMEM((all_rows, width), F32)
    short = pltpu.VMEM((all_rows, width), BF16)
    chunks = pltpu.VMEM((owners, chunk, width), BF16)
    rows_kind = (chunk_rows, LANES)
    grads, arrived, reduced, back, ln_total = pl.pallas_call(
        functools.partial(
            step_kernel, groups, owners, group, taps, size, early, total_frames
        ),
        in_specs=[in_smem] + [anywhere] * 4 + [in_vmem] * 8,
        out_specs=[in_vmem] * 5,
        out_shape=[
            jax.ShapeDtypeStruct((all_rows, width), BF16),
            jax.ShapeDtypeStruct((owners, chunk, width), BF16),
            jax.ShapeDtypeStruct((groups,) + rows_kind, BF16),
            jax.ShapeDtypeStruct(sums_shape, F32),
            jax.ShapeDtypeStruct(sums_shape, F32),
        ],
        scratch_shapes=[
            pltpu.VMEM((slots, span, width), BF16),
            pltpu.VMEM((own_rows, width), BF16),
            pltpu.VMEM(w_in.shape, BF16),
            pltpu.VMEM(w_out.shape, BF16),
            pltpu.VMEM((blocks, own_rows + span, LANES), F32),
            chunks,
            chunks,
            chunks,
            tall,
            pltpu.VMEM((all_rows, LANES), F32),
            tall,
            tall,
            short,
            pltpu.VMEM((slots * size, width), F32),
            tall,
            tall,
            short,
            short,
            pltpu.VMEM((all_rows, w_in.shape[1]), BF16),
            pltpu.VMEM((3 * size // 2, width), F32),
            pltpu.VMEM((2, SUB, width), F32),
            pltpu.VMEM((3 * size // 2, width), F32),
            pltpu.VMEM(sums_shape, F32),
            pltpu.VMEM((3,) + sums_shape, F32),
            pltpu.VMEM((3, count) + sums_shape, F32),
            pltpu.VMEM((LANES, LANES), F32),
            pltpu.VMEM((owners, 2, sides) + rows_kind, BF16),
            pltpu.VMEM((owners, sides) + rows_kind, BF16),
            pltpu.VMEM((owners, sides) + rows_kind, BF16),
            pltpu.VMEM((sides, owners) + rows_kind, BF16),
            pltpu.VMEM((owners,) + rows_kind, BF16),
            pltpu.VMEM((owners,) + rows_kind, BF16),
            pltpu.VMEM(rows_kind, BF16),
            pltpu.SemaphoreType.DMA((4,)),
            pltpu.SemaphoreType.DMA((3, count)),
            pltpu.SemaphoreType.DMA((3, count)),
            pltpu.SemaphoreType.DMA((2, owners)),
            pltpu.SemaphoreType.DMA((2, owners)),
            pltpu.SemaphoreType.DMA((owners,)),
            pltpu.SemaphoreType.DMA((owners,)),
            pltpu.SemaphoreType.DMA((2, owners)),
            pltpu.SemaphoreType.DMA((2, sides * owners)),
            pltpu.SemaphoreType.DMA((2, owners)),
            pltpu.SemaphoreType.DMA((2, groups)),
        ],
        compiler_params=pltpu.CompilerParams(
            collective_id=0, has_side_effects=True, vmem_limit_bytes=54 << 20
        ),
        cost_estimate=pl.CostEstimate(
            flops=10**10, bytes_accessed=4 * 10**7, transcendentals=0
        ),
        name="step",
    )(
        meta, *map(in_hbm, (frames.reshape(slots, span, width), upstream, w_in, w_out)),
        ln_gain[None], bn_gain[None], bn_bias[None], jnp.pad(w_dw.T, ((0, 1), (0, 0))),
        fwd, inv, spec, corr,
    )

    row_shape = jax.ShapeDtypeStruct((1, width), F32)
    out_frames, grad_frames, grad_win, grad_wo, grad_taps, grad_ln, grad_gain, grad_bias = (
        pl.pallas_call(
            functools.partial(finish_kernel, taps, per, piece),
            in_specs=[in_smem] + [in_vmem] * 5,
            out_specs=[in_vmem, anywhere] + [in_vmem] * 6,
            out_shape=[
                jax.ShapeDtypeStruct((own_rows, width), BF16),
                jax.ShapeDtypeStruct((all_rows, width), BF16),
                jax.ShapeDtypeStruct((share, w_in.shape[1]), F32),
                jax.ShapeDtypeStruct((share, width), F32),
                jax.ShapeDtypeStruct((taps, share), F32),
                jax.ShapeDtypeStruct((1, share), F32),
                row_shape,
                row_shape,
            ],
            scratch_shapes=[
                pltpu.VMEM((blocks, own_rows + span, LANES), F32),
                pltpu.VMEM((LANES, LANES), F32),
                pltpu.SemaphoreType.DMA((slots,)),
            ],
            compiler_params=pltpu.CompilerParams(vmem_limit_bytes=24 << 20),
            name="finish",
        )(meta, grads, arrived.reshape(slots, span, width), reduced, back, ln_total)
    )
    return (
        out_frames,
        grad_frames,
        grad_win,
        grad_wo,
        grad_taps.T,
        grad_ln[0],
        grad_gain[0],
        grad_bias[0],
    )


def solution(mesh):
    placed = (
        P(("dp", "bucket"), None),
        P("dp", None),
        P("dp", None),
        P(("dp", "bucket"), None),
        P(),
        P(),
        P(),
        P(),
        P(),
        P(),
    )
    return jax.shard_map(
        local,
        mesh=mesh,
        in_specs=placed,
        out_specs=(
            P(("dp", "bucket"), None),
            P(("dp", "bucket"), None),
            P("bucket", None),
            P("bucket", None),
            P("bucket", None),
            P("bucket"),
            P(),
            P(),
        ),
        check_vma=False,
    )
```

```python
import functools

import jax
import jax.numpy as jnp
import numpy as np
from jax import lax
from jax.experimental import pallas as pl
from jax.experimental.pallas import tpu as pltpu
from jax.sharding import PartitionSpec as P

EPSILON = 1e-05
LANES = 128
SUB = 8
PACK = 16
STEP_VMEM = 50 << 20
MESH = pl.DeviceIdType.MESH
BF16 = jnp.bfloat16
F32 = jnp.float32


def lane(c):
    return slice(c * LANES, (c + 1) * LANES)


def row_of(packed, first, blocks):
    return jnp.concatenate([packed[first + c : first + c + 1] for c in range(blocks)], axis=1)


def keep_live(values, lengths, span):
    position = lax.broadcasted_iota(jnp.int32, (span, values.shape[1]), 0)
    parts = [
        jnp.where(position < length, values[i * span : (i + 1) * span], 0.0)
        for i, length in enumerate(lengths)
    ]
    return jnp.concatenate(parts, axis=0)


def fold_rows(values):
    rows, width = values.shape
    return jnp.sum(values.reshape(rows // SUB, SUB, width), axis=0)


def matmul(a, b):
    return jnp.dot(a, b, preferred_element_type=F32)


def matmul_nt(a, b):
    return lax.dot_general(a, b, (((1,), (1,)), ((), ())), preferred_element_type=F32)


def matmul_tn(a, b):
    return lax.dot_general(a, b, (((0,), (0,)), ((), ())), preferred_element_type=F32)


def matmul_exact(a, b):
    return jnp.dot(a, b, preferred_element_type=F32, precision=lax.Precision.HIGHEST)


def transform_tables(span, taps, group):
    size = -(-(span + taps // 2) // (2 * PACK)) * (2 * PACK)
    half = size // 2
    freq = np.arange(half)[:, None]

    def angle(times):
        return 2.0 * np.pi * freq * np.asarray(times)[None, :] / size

    def flip(times):
        return np.where(np.asarray(times) % 2 == 0, 1.0, -1.0)

    times = np.arange(span)
    real, imag = np.cos(angle(times)), -np.sin(angle(times))
    imag[0] = flip(times)
    forward = np.concatenate([real, imag], axis=0)
    scale = np.where(np.arange(size) % half == 0, 1.0, 2.0) / size
    inverse = (forward * scale[:, None]).T
    lags = taps // 2 - np.arange(taps)
    wr, wi, wn = np.cos(angle(lags)), -np.sin(angle(lags)), np.cos(angle(lags))
    wi[0] = 0.0
    wn[0] = flip(lags)
    spectrum = np.concatenate([wr, wi, wn], axis=0)
    spectrum = np.pad(spectrum, ((0, 0), (0, 1)))
    back = -lags
    cr, cn, ci = np.cos(angle(back)), np.cos(angle(back)), -np.sin(angle(back))
    cn[0] = flip(back)
    ci[0] = 0.0
    both = np.concatenate([scale[:half], scale[half:], scale[half:]])
    correlate = (np.concatenate([cr, cn, ci], axis=0) * both[:, None]).T
    correlate = np.pad(correlate, ((0, 1), (0, 0)))
    eye = np.eye(group)
    return (
        size,
        jnp.asarray(np.kron(eye, forward), BF16),
        jnp.asarray(np.kron(eye, inverse), BF16),
        jnp.asarray(spectrum, F32),
        jnp.asarray(correlate, F32),
    )


def chunk_bounds(own_rows, pairs, span, loaders):
    rows = [min(pairs * span, (own_rows - b * pairs) // (loaders - b)) for b in range(loaders)]
    return [-(-r // PACK) * PACK for r in rows]


def tables_kernel(slots, lens_ref, owners_ref, meta_ref, counts):
    me = lax.axis_index("bucket")
    loaders = lens_ref.shape[1] // slots
    pairs = slots // loaders

    def look(b, start):
        meta_ref[2, b] = start
        for j in range(slots):
            at = b * slots + j
            start = start + jnp.where(owners_ref[0, at] == me, lens_ref[0, at], 0)
        return start

    lax.fori_loop(0, loaders, look, jnp.int32(0))

    def clear(i, carry):
        counts[i] = 0
        return carry

    lax.fori_loop(0, loaders, clear, 0)

    def place(i, carry):
        owner = owners_ref[0, me * slots + i]
        rank = counts[owner]
        counts[owner] = rank + 1
        at = owner * pairs + rank
        meta_ref[0, at] = lens_ref[0, me * slots + i]
        meta_ref[1, at] = i
        return carry

    lax.fori_loop(0, slots, place, 0)


def reducer(groups, owners, dp, me, src, out, refs):
    first, first_sum, second, second_sum, twin, twin_sum, third, mine = refs[:8]
    core_sems, pair_sems, twin_sems, row_sems, all_sems = refs[8:]
    sides = groups // 2
    core, side = lax.rem(dp, 2), dp // 2
    partner = side * 2 + (1 - core)

    def remote(source, target, sems, i, j, device):
        return pltpu.make_async_remote_copy(
            src_ref=source,
            dst_ref=target,
            send_sem=sems.at[0, i],
            recv_sem=sems.at[1, j],
            device_id=device,
            device_id_type=MESH,
        )

    def bucket_of(i):
        return lax.rem(me + 1 + i, owners)

    def swap(i):
        bucket = bucket_of(i)
        return remote(src.at[bucket, 1 - core], first.at[bucket], core_sems, i, i, (partner, me))

    def to_side(i, n, arriving):
        bucket = bucket_of(i)
        other = lax.rem(side + n, sides)
        slot = other if arriving else side
        return remote(
            first_sum.at[bucket, other], second.at[slot, bucket], pair_sems,
            n * owners + i, slot * owners + i, (other * 2 + core, me),
        )

    near = lax.rem(me, 2)
    mate = me + 1 - 2 * near
    pairs = owners // 2

    def pair_of(i):
        return lax.rem(me // 2 + 1 + i, pairs)

    def to_mate(i):
        pair = pair_of(i)
        return remote(second_sum.at[pair * 2 + 1 - near], twin.at[pair], twin_sems, i, i, (dp, mate))

    def to_owner(i, arriving):
        pair = lax.rem(me // 2 + i, pairs)
        slot = pair if arriving else me // 2
        return remote(
            twin_sum.at[pair], third.at[slot], row_sems, i, slot, (dp, pair * 2 + near)
        )

    def to_group(i, arriving):
        other = lax.rem(dp + i, groups)
        device = other if arriving else dp
        slot = lax.rem(device, 2) * sides + device // 2
        return remote(mine, out.at[slot], all_sems, i, slot, (other, me))

    def loop(low, high, body):
        def step(i, carry):
            body(i)
            return carry

        lax.fori_loop(low, high, step, 0)

    def add_first(i):
        bucket = bucket_of(i)
        swap(i).wait_recv()
        total = src[bucket, core].astype(F32) + first[bucket].astype(F32)
        first_sum[bucket] = total.astype(BF16)
        for n in range(1, sides):
            to_side(i, n, False).start()

    def add_second(i):
        bucket = bucket_of(i)
        total = first_sum[bucket, side].astype(F32)
        for n in range(1, sides):
            to_side(i, n, True).wait_recv()
            total = total + second[lax.rem(side + n, sides), bucket].astype(F32)
        second_sum[bucket] = total.astype(BF16)

    def add_twin(i):
        pair = pair_of(i)
        to_mate(i).wait_recv()
        total = second_sum[pair * 2 + near].astype(F32) + twin[pair].astype(F32)
        twin_sum[pair] = total.astype(BF16)

    def twin_and_send(i):
        add_twin(i)
        to_owner(i + 1, False).start()

    def stage_swap():
        loop(0, owners, lambda i: swap(i).start())

    def stage_side():
        loop(0, owners, add_first)

    def stage_mate():
        loop(0, owners, add_second)
        loop(0, pairs, lambda i: to_mate(i).start())

    def stage_owner():
        loop(0, pairs - 1, twin_and_send)
        add_twin(pairs - 1)
        third[me // 2] = twin_sum[me // 2]

    def stage_group():
        loop(1, pairs, lambda i: to_owner(i, True).wait_recv())
        total = lax.fori_loop(
            1, pairs, lambda i, t: t + third[i].astype(F32), third[0].astype(F32)
        )
        mine[...] = total.astype(BF16)
        loop(1, groups, lambda i: to_group(i, False).start())
        out[core * sides + side] = mine[...]

    def stage_end():
        loop(1, groups, lambda i: to_group(i, True).wait_recv())

        def first_sent(i):
            swap(i).wait_send()
            for n in range(1, sides):
                to_side(i, n, False).wait_send()

        loop(0, owners, first_sent)
        loop(0, pairs, lambda i: to_mate(i).wait_send())
        loop(1, pairs, lambda i: to_owner(i, False).wait_send())
        loop(1, groups, lambda i: to_group(i, False).wait_send())

    return stage_swap, stage_side, stage_mate, stage_owner, stage_group, stage_end


def step_kernel(
    groups, owners, group, taps, size, early, early_out, late_out, bounds, total_frames,
    meta, *refs,
):
    sources, refs = refs[:12], refs[12:]
    grads_ref, arrived_ref, reduced_ref, reduced_out_ref, back_ref, ln_ref = refs[:6]
    targets, refs = refs[6:18], refs[18:]
    up, w_dw_ref, spec_ref, frames, w_in_ref, gain_ref, fwd_ref, inv_ref = targets[:8]
    w_out_ref, bn_gain_ref, bn_bias_ref, corr_ref = targets[8:]
    (
    stage, outgoing, arrive, outbuf,
    normed_s, inverse_s, linear_s, gate_s, h_s, spect_s, conv_s, fac_s, sw_s, dy_s, ga_s,
    w_taps, wspec, acc, xacc, tot, parts, mids, slots_a, slots_b, flat,
    packed, packed_out, local_sems, up_send, up_recv, out_send, out_recv,
    a_send, a_recv, b_send, b_recv, *reduce_refs,
    ) = refs
    dp, me = lax.axis_index("dp"), lax.axis_index("bucket")
    slot_count, span, width = frames.shape
    all_rows = slot_count * span
    own_rows = up.shape[0]
    blocks = width // LANES
    wide = w_in_ref.shape[1] // LANES
    chunk = all_rows // owners
    pairs = slot_count // owners
    steps = slot_count // group
    held = group // pairs
    grows = group * span
    half = size // 2
    far = owners // 2
    barrier = pltpu.get_barrier_semaphore()

    def loop(low, high, body):
        def step(i, carry):
            body(i)
            return carry

        lax.fori_loop(low, high, step, 0)

    def peer_of(m):
        bits = range((owners - 1).bit_length())
        return sum(lax.rem(me // 2**k + m // 2**k, 2) * 2**k for k in bits)

    def greet_group(i):
        pl.semaphore_signal(
            barrier, inc=1, device_id=(lax.rem(dp + i, groups), me), device_id_type=MESH
        )

    def greet_owner(m):
        pl.semaphore_signal(barrier, inc=1, device_id=(dp, peer_of(m)), device_id_type=MESH)

    loop(1, groups, greet_group)
    loop(1, owners, greet_owner)
    loads = [
        pltpu.make_async_copy(source, target, local_sems.at[n])
        for n, (source, target) in enumerate(zip(sources, targets))
    ]
    for load in loads:
        load.start()

    loads[0].wait()
    for c in range(blocks):
        stage[c, :own_rows] = up[:, lane(c)].astype(F32)
        stage[c, own_rows:] = jnp.zeros((chunk, LANES), F32)

    def lay_out(b):
        start = meta[2, b]
        for c in range(blocks):
            outgoing[b, :, lane(c)] = stage[c, pl.ds(start, chunk)].astype(BF16)

    loop(0, owners, lay_out)
    arrive[me] = outgoing[me]

    def sized(index, body):
        for rows in sorted(set(bounds)):
            low = bounds.index(rows)
            high = low + bounds.count(rows)

            @pl.when(jnp.logical_and(index >= low, index < high))
            def _():
                body(rows)

    def up_copy(m, part, rows, arriving):
        peer = peer_of(m)
        slot = peer if arriving else me
        span_of = pl.ds(0, early) if part == 0 else pl.ds(early, rows - early)
        return pltpu.make_async_remote_copy(
            src_ref=outgoing.at[peer, span_of],
            dst_ref=arrive.at[slot, span_of],
            send_sem=up_send.at[part, m],
            recv_sem=up_recv.at[part, m],
            device_id=(dp, peer),
            device_id_type=MESH,
        )

    cuts = (0, early_out, late_out, chunk)

    def out_copy(m, part, rows, arriving):
        peer = peer_of(m)
        slot = peer if arriving else me
        low, high = cuts[part], min(cuts[part + 1], rows)
        return pltpu.make_async_remote_copy(
            src_ref=outbuf.at[peer, pl.ds(low, high - low)],
            dst_ref=arrived_ref.at[slot, pl.ds(low, high - low)],
            send_sem=out_send.at[part, m],
            recv_sem=out_recv.at[part, m],
            device_id=(dp, peer),
            device_id_type=MESH,
        )

    def each_out(loader, m, part, arriving, use):
        def body(rows):
            if rows > cuts[part]:
                use(out_copy(m, part, rows, arriving))

        sized(loader, body)

    def start_out(low, high, part):
        loop(
            low,
            high,
            lambda j: each_out(me, owners - 1 - j, part, False, lambda copy: copy.start()),
        )

    def start_up(part):
        def body(j):
            m = owners - 1 - j
            if part == 0:
                up_copy(m, 0, None, False).start()
            else:
                sized(peer_of(m), lambda rows: up_copy(m, 1, rows, False).start())

        loop(0, owners - 1, body)

    def a_copy(n, i, arriving):
        other = lax.rem(dp + i, groups)
        slot = lax.rem(dp + groups - i, groups) if arriving else dp
        return pltpu.make_async_remote_copy(
            src_ref=parts.at[n],
            dst_ref=slots_a.at[n, slot],
            send_sem=a_send.at[n, i],
            recv_sem=a_recv.at[n, i],
            device_id=(other, me),
            device_id_type=MESH,
        )

    def b_copy(n, m, arriving):
        peer = peer_of(m)
        slot = peer if arriving else me
        return pltpu.make_async_remote_copy(
            src_ref=mids.at[n],
            dst_ref=slots_b.at[n, slot],
            send_sem=b_send.at[n, m],
            recv_sem=b_recv.at[n, m],
            device_id=(dp, peer),
            device_id_type=MESH,
        )

    def sum_start(n):
        for k in range(2):
            row = jnp.sum(acc[k], axis=0, keepdims=True)
            for c in range(blocks):
                parts[n, k * blocks + c : k * blocks + c + 1] = row[:, lane(c)]
        loop(1, groups, lambda i: a_copy(n, i, False).start())
        slots_a[n, dp] = parts[n]

    def sum_middle(n):
        loop(1, groups, lambda i: a_copy(n, i, True).wait_recv())
        mids[n] = lax.fori_loop(1, groups, lambda i, t: t + slots_a[n, i], slots_a[n, 0])
        loop(0, owners - 1, lambda j: b_copy(n, owners - 1 - j, False).start())
        slots_b[n, me] = mids[n]

    def sum_finish(n):
        loop(1, owners, lambda m: b_copy(n, m, True).wait_recv())
        return lax.fori_loop(1, owners, lambda i, t: t + slots_b[n, i], slots_b[n, 0])

    loads[1].wait()
    loads[2].wait()
    w_taps[...] = jnp.zeros_like(w_taps)
    w_taps[:taps] = w_dw_ref[...]
    wspec[...] = matmul_exact(spec_ref[...], w_taps[...])
    acc[...] = jnp.zeros_like(acc)
    pl.semaphore_wait(barrier, groups + owners - 2)
    start_up(0)
    for load in loads[3:8]:
        load.wait()

    def rows_of(i):
        return pl.ds(pl.multiple_of(i * grows, PACK), grows)

    def spec_rows(i):
        return pl.ds(pl.multiple_of(i * group * size, PACK), group * size)

    def lengths_of(i):
        return [meta[0, i * group + u] for u in range(group)]

    def packing(lengths):
        column = lax.broadcasted_iota(jnp.int32, (1, grows), 1)
        target = jnp.full((1, grows), -1, jnp.int32)
        for u in range(group):
            first = (u // pairs) * chunk + sum(lengths[u - u % pairs : u], jnp.int32(0))
            at = column - u * span
            live = jnp.logical_and(at >= 0, at < lengths[u])
            target = jnp.where(live, at + first, target)
        row = lax.broadcasted_iota(jnp.int32, (grows, grows), 0)
        return jnp.where(row == target, 1.0, 0.0).astype(BF16)

    def forward(i):
        rows = rows_of(i)
        lengths = lengths_of(i)
        values = jnp.concatenate(
            [frames[meta[1, i * group + u]] for u in range(group)], axis=0
        ).astype(F32)
        centred = values - jnp.mean(values, axis=1, keepdims=True)
        inverse = lax.rsqrt(jnp.mean(centred * centred, axis=1, keepdims=True) + EPSILON)
        normed = centred * inverse
        h = (normed * gain_ref[...]).astype(BF16)
        projected = matmul(h, w_in_ref[...])
        linear, gate = projected[:, :width], jax.nn.sigmoid(projected[:, width:])
        normed_s[rows] = normed
        inverse_s[rows] = jnp.broadcast_to(inverse, (grows, LANES))
        linear_s[rows] = linear
        gate_s[rows] = gate
        h_s[rows] = h
        gated = keep_live(linear * gate, lengths, span).astype(BF16)
        spect = matmul(fwd_ref[...], gated)
        spect_s[spec_rows(i)] = spect
        wr, wi, wn = wspec[:half], wspec[half : 2 * half], wspec[2 * half :]
        mixed = []
        for u in range(group):
            re = spect[u * size : u * size + half]
            im = spect[u * size + half : (u + 1) * size]
            mixed.append((wr * re - wi * im).astype(BF16))
            mixed.append((wn * im + wi * re).astype(BF16))
        conv = matmul(inv_ref[...], jnp.concatenate(mixed, axis=0))
        conv_s[rows] = conv
        masked = keep_live(conv, lengths, span)
        acc[0] += fold_rows(masked)
        acc[1] += fold_rows(masked * masked)

    loop(0, steps, forward)
    sum_start(0)
    sum_middle(0)
    for load in loads[8:]:
        load.wait()
    tot[...] = sum_finish(0)
    start_up(1)
    centre = row_of(tot, 0, blocks) / total_frames
    variance = row_of(tot, blocks, blocks) / total_frames - centre * centre
    bn_inverse = lax.rsqrt(variance + EPSILON)
    acc[...] = jnp.zeros_like(acc)
    bn_gain, bn_bias = bn_gain_ref[...], bn_bias_ref[...]

    def swish(i):
        rows = rows_of(i)
        bn_normed = (conv_s[rows] - centre) * bn_inverse
        conv_s[rows] = bn_normed
        bn = bn_normed * bn_gain + bn_bias
        sig = jax.nn.sigmoid(bn)
        swished = (bn * sig).astype(BF16)
        sw_s[rows] = swished
        fac_s[rows] = sig * (1.0 + bn * (1.0 - sig))
        out = matmul(swished, w_out_ref[...]).astype(BF16)
        out = matmul(packing(lengths_of(i)), out).astype(BF16)
        for r in range(held):
            outbuf[i * held + r] = out[r * chunk : (r + 1) * chunk]

    loop(0, steps, swish)

    @pl.when(me >= far)
    def _():
        start_out(0, far, 0)

    def middle(t):
        m = lax.rem(owners - t * held, owners)
        i = peer_of(m) // held
        rows = rows_of(i)
        lengths = lengths_of(i)
        for r in range(held):
            owner = i * held + r
            bits = range((owners - 1).bit_length())
            gap = sum(lax.rem(me // 2**k + owner // 2**k, 2) * 2**k for k in bits)

            @pl.when(owner != me)
            def _():
                up_copy(gap, 0, None, True).wait_recv()
                sized(me, lambda rows: up_copy(gap, 1, rows, True).wait_recv())

        pieces = []
        position = lax.broadcasted_iota(jnp.int32, (chunk, width), 0)
        for r in range(held):
            total = sum(lengths[r * pairs : (r + 1) * pairs], jnp.int32(0))
            came = arrive[i * held + r].astype(F32)
            pieces.append(jnp.where(position < total, came, 0.0).astype(BF16))
        dy = matmul_tn(packing(lengths), jnp.concatenate(pieces, axis=0)).astype(BF16)
        dy_s[rows] = dy
        grad_bn = matmul_nt(dy, w_out_ref[...]) * fac_s[rows]
        fac_s[rows] = grad_bn
        acc[0] += fold_rows(grad_bn)
        acc[1] += fold_rows(grad_bn * conv_s[rows])

    loop(0, steps, middle)
    sum_start(1)
    sum_middle(1)

    arrived_ref[me] = outbuf[me]

    share = width // owners
    per, per_out = -(-wide // groups), -(-blocks // groups)
    piece = share // groups
    sides = groups // 2
    in_stages = reducer(groups, owners, dp, me, packed, reduced_ref, reduce_refs[:13])
    out_stages = reducer(groups, owners, dp, me, packed_out, reduced_out_ref, reduce_refs[13:])

    def put(target, count, j, section, block):
        q, r = section // count, section % count
        target[j, q // sides, q % sides, r * share : (r + 1) * share] = block.astype(BF16)

    if per_out * groups != blocks:
        packed_out[...] = jnp.zeros_like(packed_out)
    if per * groups != wide or packed.shape[3] != per * share + piece:
        packed[...] = jnp.zeros_like(packed)
    for c in range(blocks):
        grad = matmul_tn(sw_s[:, lane(c)], dy_s[...])
        for n in range(LANES // share):
            j = c * (LANES // share) + n
            for s in range(blocks):
                put(packed_out, per_out, j, s, grad[n * share : (n + 1) * share, lane(s)])
    out_stages[0]()
    back_ref[...] = sum_finish(1)

    @pl.when(me < far)
    def _():
        start_out(0, far, 0)

    start_out(0, far, 1)
    start_out(far, owners - 1, 0)
    start_out(far, owners - 1, 1)
    bias_mean = row_of(back_ref, 0, blocks) / total_frames
    gain_mean = row_of(back_ref, blocks, blocks) / total_frames
    scale = bn_gain * bn_inverse
    xacc[...] = jnp.zeros_like(xacc)

    def backward(i):
        rows = rows_of(i)
        lengths = lengths_of(i)
        grad_conv = scale * (fac_s[rows] - bias_mean - conv_s[rows] * gain_mean)
        grad_conv = keep_live(grad_conv, lengths, span).astype(BF16)
        spect = matmul(fwd_ref[...], grad_conv)
        saved = spect_s[spec_rows(i)]
        wr, wi, wn = wspec[:half], wspec[half : 2 * half], wspec[2 * half :]
        mixed, terms = [], [None] * 3
        for u in range(group):
            re = spect[u * size : u * size + half]
            im = spect[u * size + half : (u + 1) * size]
            sre = saved[u * size : u * size + half]
            sim = saved[u * size + half : (u + 1) * size]
            mixed.append((wr * re + wi * im).astype(BF16))
            mixed.append((wn * im - wi * re).astype(BF16))
            new = (re * sre, im * sim, re * sim - im * sre)
            terms = [b if a is None else a + b for a, b in zip(terms, new)]
        for n in range(3):
            xacc[n * half : (n + 1) * half] += terms[n]
        grad_gated = matmul(inv_ref[...], jnp.concatenate(mixed, axis=0))
        grad_gated = keep_live(grad_gated, lengths, span)
        gate = gate_s[rows]
        left = grad_gated * gate
        ga_s[rows, :width] = left.astype(BF16)
        ga_s[rows, width:] = (left * linear_s[rows] * (1.0 - gate)).astype(BF16)

    loop(0, steps // 2, backward)
    out_stages[1]()
    loop(steps // 2, steps, backward)
    out_stages[2]()
    grad_taps = matmul_exact(corr_ref[...], xacc[...])
    flat[...] = jnp.zeros_like(flat)
    for c in range(blocks):
        grad = matmul_tn(h_s[:, lane(c)], ga_s[...])
        flat[: taps + 1] = grad_taps[:, lane(c)]
        turned = flat[...].T.astype(BF16)
        for n in range(LANES // share):
            j = c * (LANES // share) + n
            for s in range(wide):
                put(packed, per, j, s, grad[n * share : (n + 1) * share, lane(s)])
            for q in range(groups):
                packed[j, q // sides, q % sides, per * share : per * share + piece] = turned[
                    n * share + q * piece : n * share + (q + 1) * piece
                ]
    in_stages[0]()
    acc[...] = jnp.zeros_like(acc)

    def last(i):
        rows = rows_of(i)
        lengths = lengths_of(i)
        grad_h = matmul_nt(ga_s[rows], w_in_ref[...])
        normed, inverse = normed_s[rows], inverse_s[rows][:, :1]
        acc[0] += fold_rows(grad_h * normed)
        scaled = grad_h * gain_ref[...]
        inner_mean = jnp.mean(scaled * normed, axis=1, keepdims=True)
        grad_x = inverse * (scaled - jnp.mean(scaled, axis=1, keepdims=True) - normed * inner_mean)
        grads_ref[rows] = keep_live(grad_x, lengths, span).astype(BF16)

    loop(0, steps // 4, last)
    in_stages[1]()
    out_stages[3]()
    loop(steps // 4, steps // 2, last)
    in_stages[2]()
    loop(steps // 2, steps, last)
    in_stages[3]()
    start_out(0, owners - 1, 2)
    sum_start(2)
    out_stages[4]()
    sum_middle(2)
    in_stages[4]()
    ln_ref[...] = sum_finish(2)
    in_stages[5]()
    out_stages[5]()

    def finish_copies(m):
        up_copy(m, 0, None, False).wait_send()
        sized(peer_of(m), lambda rows: up_copy(m, 1, rows, False).wait_send())
        for part in range(3):
            each_out(peer_of(m), m, part, True, lambda copy: copy.wait_recv())
            each_out(me, m, part, False, lambda copy: copy.wait_send())
        for n in range(3):
            b_copy(n, m, False).wait_send()

    loop(1, owners, finish_copies)

    def finish_sums(i):
        for n in range(3):
            a_copy(n, i, False).wait_send()

    loop(1, groups, finish_sums)


def finish_kernel(
    taps, per, per_out, piece, bounds,
    meta, grads_ref, arrived_ref, reduced_ref, reduced_out_ref, back_ref, ln_ref,
    out_ref, grad_frames_ref, win_ref, wout_ref, taps_ref, ln_out_ref, gain_ref, bias_ref,
    stage, flat, sems,
):
    me = lax.axis_index("bucket")
    owners, chunk, width = arrived_ref.shape
    own_rows = out_ref.shape[0]
    blocks = width // LANES
    share = win_ref.shape[0]
    wide = win_ref.shape[1] // LANES
    slots = sems.shape[0]
    span = grads_ref.shape[0] // slots

    def row_copy(i):
        source = pl.ds(pl.multiple_of(i * span, PACK), span)
        target = pl.ds(pl.multiple_of(meta[1, i] * span, PACK), span)
        return pltpu.make_async_copy(
            grads_ref.at[source], grad_frames_ref.at[target], sems.at[i]
        )

    def start(i, carry):
        row_copy(i).start()
        return carry

    lax.fori_loop(0, slots, start, 0)
    for b in range(owners):
        begin = meta[2, b]
        for c in range(blocks):
            stage[c, pl.ds(begin, bounds[b])] = arrived_ref[b, : bounds[b], lane(c)].astype(F32)
    for c in range(blocks):
        out_ref[:, lane(c)] = stage[c, :own_rows].astype(BF16)

    def section(source, count, s):
        q, r = s // count, s % count
        return source[q, r * share : (r + 1) * share].astype(F32)

    for c in range(blocks):
        wout_ref[:, lane(c)] = section(reduced_out_ref, per_out, c)
    for c in range(wide):
        win_ref[:, lane(c)] = section(reduced_ref, per, c)
    flat[...] = jnp.zeros_like(flat)
    for q in range(reduced_ref.shape[0]):
        flat[q * piece : (q + 1) * piece] = reduced_ref[
            q, per * share : per * share + piece
        ].astype(F32)
    taps_ref[...] = flat[...].T[:taps, :share]
    row = jnp.zeros((1, share), F32)
    for j in range(owners):
        c, n = j * share // LANES, j * share % LANES
        row = jnp.where(me == j, ln_ref[c : c + 1, n : n + share], row)
    ln_out_ref[...] = row
    bias_ref[...] = row_of(back_ref, 0, blocks)
    gain_ref[...] = row_of(back_ref, blocks, blocks)

    def wait(i, carry):
        row_copy(i).wait()
        return carry

    lax.fori_loop(0, slots, wait, 0)


def in_hbm(array):
    return pltpu.with_memory_space_constraint(array, pltpu.HBM)


def local(frames, lengths, owner_ids, upstream, ln_gain, w_in, w_dw, bn_gain, bn_bias, w_out):
    groups, owners = lax.axis_size("dp"), lax.axis_size("bucket")
    all_rows, width = frames.shape
    taps = w_dw.shape[1]
    slots = lengths.shape[1] // owners
    span = all_rows // slots
    pairs = slots // owners
    own_rows = upstream.shape[0]
    blocks = width // LANES
    wide = w_in.shape[1] // LANES
    total_frames = float(own_rows * owners * groups)
    in_vmem = pl.BlockSpec(memory_space=pltpu.VMEM)
    in_smem = pl.BlockSpec(memory_space=pltpu.SMEM)
    anywhere = pl.BlockSpec(memory_space=pl.ANY)
    group = pairs * max(1, 4 // pairs)
    size, fwd, inv, spec, corr = transform_tables(span, taps, group)
    chunk = pairs * span
    bounds = chunk_bounds(own_rows, pairs, span, owners)
    early = max(PACK, chunk // 3 // PACK * PACK)
    early_out = max(PACK, min(chunk * 5 // 12 // PACK * PACK, bounds[0] - PACK))
    late_out = max(early_out + PACK, chunk * 3 // 4 // PACK * PACK)
    share = width // owners
    per, per_out = -(-wide // groups), -(-blocks // groups)
    piece = share // groups
    sides = groups // 2
    rows_in = (per * share + -(-piece // PACK) * PACK, LANES)
    rows_out = (per_out * share, LANES)

    meta = pl.pallas_call(
        functools.partial(tables_kernel, slots),
        in_specs=[in_smem, in_smem],
        out_specs=in_smem,
        out_shape=jax.ShapeDtypeStruct((3, slots), jnp.int32),
        scratch_shapes=[pltpu.SMEM((owners,), jnp.int32)],
        compiler_params=pltpu.CompilerParams(vmem_limit_bytes=1 << 20),
        name="tables",
    )(in_hbm(lengths), in_hbm(owner_ids))

    operands = (
        upstream, w_dw.T, spec, frames.reshape(slots, span, width), w_in, ln_gain[None], fwd, inv,
        w_out, bn_gain[None], bn_bias[None], corr,
    )
    sums_shape = (2 * blocks, LANES)
    tall = pltpu.VMEM((all_rows, width), F32)
    short = pltpu.VMEM((all_rows, width), BF16)
    chunks = pltpu.VMEM((owners, chunk, width), BF16)

    def reduce_scratch(kind):
        return [
            pltpu.VMEM((owners, sides) + kind, BF16),
            pltpu.VMEM((owners, sides) + kind, BF16),
            pltpu.VMEM((sides, owners) + kind, BF16),
            pltpu.VMEM((owners,) + kind, BF16),
            pltpu.VMEM((owners // 2,) + kind, BF16),
            pltpu.VMEM((owners // 2,) + kind, BF16),
            pltpu.VMEM((owners // 2,) + kind, BF16),
            pltpu.VMEM(kind, BF16),
            pltpu.SemaphoreType.DMA((2, owners)),
            pltpu.SemaphoreType.DMA((2, sides * owners)),
            pltpu.SemaphoreType.DMA((2, owners // 2)),
            pltpu.SemaphoreType.DMA((2, owners // 2)),
            pltpu.SemaphoreType.DMA((2, groups)),
        ]

    grads, arrived, reduced, reduced_out, back, ln_total = pl.pallas_call(
        functools.partial(
            step_kernel,
            groups, owners, group, taps, size, early, early_out, late_out, bounds,
            total_frames,
        ),
        in_specs=[in_smem] + [anywhere] * 12,
        out_specs=[in_vmem] * 6,
        out_shape=[
            jax.ShapeDtypeStruct((all_rows, width), BF16),
            jax.ShapeDtypeStruct((owners, chunk, width), BF16),
            jax.ShapeDtypeStruct((groups,) + rows_in, BF16),
            jax.ShapeDtypeStruct((groups,) + rows_out, BF16),
            jax.ShapeDtypeStruct(sums_shape, F32),
            jax.ShapeDtypeStruct(sums_shape, F32),
        ],
        scratch_shapes=[pltpu.VMEM(operand.shape, operand.dtype) for operand in operands]
        + [
            pltpu.VMEM((blocks, own_rows + chunk, LANES), F32),
            chunks,
            chunks,
            chunks,
            tall,
            pltpu.VMEM((all_rows, LANES), F32),
            tall,
            tall,
            short,
            pltpu.VMEM((slots * size, width), F32),
            tall,
            tall,
            short,
            short,
            pltpu.VMEM((all_rows, w_in.shape[1]), BF16),
            pltpu.VMEM((taps + 1, width), F32),
            pltpu.VMEM((3 * size // 2, width), F32),
            pltpu.VMEM((2, SUB, width), F32),
            pltpu.VMEM((3 * size // 2, width), F32),
            pltpu.VMEM(sums_shape, F32),
            pltpu.VMEM((3,) + sums_shape, F32),
            pltpu.VMEM((3,) + sums_shape, F32),
            pltpu.VMEM((3, groups) + sums_shape, F32),
            pltpu.VMEM((3, owners) + sums_shape, F32),
            pltpu.VMEM((LANES, LANES), F32),
            pltpu.VMEM((owners, 2, sides) + rows_in, BF16),
            pltpu.VMEM((owners, 2, sides) + rows_out, BF16),
            pltpu.SemaphoreType.DMA((12,)),
            pltpu.SemaphoreType.DMA((2, owners)),
            pltpu.SemaphoreType.DMA((2, owners)),
            pltpu.SemaphoreType.DMA((3, owners)),
            pltpu.SemaphoreType.DMA((3, owners)),
            pltpu.SemaphoreType.DMA((3, groups)),
            pltpu.SemaphoreType.DMA((3, groups)),
            pltpu.SemaphoreType.DMA((3, owners)),
            pltpu.SemaphoreType.DMA((3, owners)),
        ]
        + reduce_scratch(rows_in)
        + reduce_scratch(rows_out),
        compiler_params=pltpu.CompilerParams(
            collective_id=0, has_side_effects=True, vmem_limit_bytes=STEP_VMEM
        ),
        cost_estimate=pl.CostEstimate(
            flops=10**10, bytes_accessed=4 * 10**7, transcendentals=0
        ),
        name="step",
    )(meta, *map(in_hbm, operands))

    row_shape = jax.ShapeDtypeStruct((1, width), F32)
    out_frames, grad_frames, grad_win, grad_wo, grad_taps, grad_ln, grad_gain, grad_bias = (
        pl.pallas_call(
            functools.partial(finish_kernel, taps, per, per_out, piece, bounds),
            in_specs=[in_smem] + [in_vmem] * 6,
            out_specs=[in_vmem, anywhere] + [in_vmem] * 6,
            out_shape=[
                jax.ShapeDtypeStruct((own_rows, width), BF16),
                jax.ShapeDtypeStruct((all_rows, width), BF16),
                jax.ShapeDtypeStruct((share, w_in.shape[1]), F32),
                jax.ShapeDtypeStruct((share, width), F32),
                jax.ShapeDtypeStruct((taps, share), F32),
                jax.ShapeDtypeStruct((1, share), F32),
                row_shape,
                row_shape,
            ],
            scratch_shapes=[
                pltpu.VMEM((blocks, own_rows + chunk, LANES), F32),
                pltpu.VMEM((LANES, LANES), F32),
                pltpu.SemaphoreType.DMA((slots,)),
            ],
            compiler_params=pltpu.CompilerParams(vmem_limit_bytes=8 << 20),
            name="finish",
        )(meta, grads, arrived, reduced, reduced_out, back, ln_total)
    )
    return (
        out_frames,
        grad_frames,
        grad_win,
        grad_wo,
        grad_taps.T,
        grad_ln[0],
        grad_gain[0],
        grad_bias[0],
    )


def solution(mesh):
    placed = (
        P(("dp", "bucket"), None),
        P("dp", None),
        P("dp", None),
        P(("dp", "bucket"), None),
        P(),
        P(),
        P(),
        P(),
        P(),
        P(),
    )
    return jax.shard_map(
        local,
        mesh=mesh,
        in_specs=placed,
        out_specs=(
            P(("dp", "bucket"), None),
            P(("dp", "bucket"), None),
            P("bucket", None),
            P("bucket", None),
            P("bucket", None),
            P("bucket"),
            P(),
            P(),
        ),
        check_vma=False,
    )
```

```python
import functools

import jax
import jax.numpy as jnp
import numpy as np
from jax import lax
from jax.experimental import pallas as pl
from jax.experimental.pallas import tpu as pltpu
from jax.sharding import PartitionSpec as P

EPSILON = 1e-05
LANES = 128
SUB = 8
PACK = 16
STEP_VMEM = 50 << 20
MESH = pl.DeviceIdType.MESH
BF16 = jnp.bfloat16
F32 = jnp.float32


def lane(c):
    return slice(c * LANES, (c + 1) * LANES)


def row_of(packed, first, blocks):
    return jnp.concatenate([packed[first + c : first + c + 1] for c in range(blocks)], axis=1)


def keep_live(values, lengths, span):
    position = lax.broadcasted_iota(jnp.int32, (span, values.shape[1]), 0)
    parts = [
        jnp.where(position < length, values[i * span : (i + 1) * span], 0.0)
        for i, length in enumerate(lengths)
    ]
    return jnp.concatenate(parts, axis=0)


def fold_rows(values):
    rows, width = values.shape
    return jnp.sum(values.reshape(rows // SUB, SUB, width), axis=0)


def matmul(a, b):
    return jnp.dot(a, b, preferred_element_type=F32)


def matmul_nt(a, b):
    return lax.dot_general(a, b, (((1,), (1,)), ((), ())), preferred_element_type=F32)


def matmul_tn(a, b):
    return lax.dot_general(a, b, (((0,), (0,)), ((), ())), preferred_element_type=F32)


def matmul_exact(a, b):
    return jnp.dot(a, b, preferred_element_type=F32, precision=lax.Precision.HIGHEST)


def transform_tables(span, taps, group):
    size = -(-(span + taps // 2) // (2 * PACK)) * (2 * PACK)
    half = size // 2
    freq = np.arange(half)[:, None]

    def angle(times):
        return 2.0 * np.pi * freq * np.asarray(times)[None, :] / size

    def flip(times):
        return np.where(np.asarray(times) % 2 == 0, 1.0, -1.0)

    times = np.arange(span)
    real, imag = np.cos(angle(times)), -np.sin(angle(times))
    imag[0] = flip(times)
    forward = np.concatenate([real, imag], axis=0)
    scale = np.where(np.arange(size) % half == 0, 1.0, 2.0) / size
    inverse = (forward * scale[:, None]).T
    lags = taps // 2 - np.arange(taps)
    wr, wi, wn = np.cos(angle(lags)), -np.sin(angle(lags)), np.cos(angle(lags))
    wi[0] = 0.0
    wn[0] = flip(lags)
    spectrum = np.concatenate([wr, wi, wn], axis=0)
    spectrum = np.pad(spectrum, ((0, 0), (0, 1)))
    back = -lags
    cr, cn, ci = np.cos(angle(back)), np.cos(angle(back)), -np.sin(angle(back))
    cn[0] = flip(back)
    ci[0] = 0.0
    both = np.concatenate([scale[:half], scale[half:], scale[half:]])
    correlate = (np.concatenate([cr, cn, ci], axis=0) * both[:, None]).T
    correlate = np.pad(correlate, ((0, 1), (0, 0)))
    eye = np.eye(group)
    return (
        size,
        jnp.asarray(np.kron(eye, forward), BF16),
        jnp.asarray(np.kron(eye, inverse), BF16),
        jnp.asarray(spectrum, F32),
        jnp.asarray(correlate, F32),
    )


def chunk_bounds(own_rows, pairs, span, loaders):
    rows = [min(pairs * span, (own_rows - b * pairs) // (loaders - b)) for b in range(loaders)]
    return [-(-r // PACK) * PACK for r in rows]


def tables_kernel(slots, lens_ref, owners_ref, meta_ref, counts):
    me = lax.axis_index("bucket")
    loaders = lens_ref.shape[1] // slots
    pairs = slots // loaders

    def look(b, start):
        meta_ref[2, b] = start
        for j in range(slots):
            at = b * slots + j
            start = start + jnp.where(owners_ref[0, at] == me, lens_ref[0, at], 0)
        return start

    lax.fori_loop(0, loaders, look, jnp.int32(0))

    def clear(i, carry):
        counts[i] = 0
        return carry

    lax.fori_loop(0, loaders, clear, 0)

    def place(i, carry):
        owner = owners_ref[0, me * slots + i]
        rank = counts[owner]
        counts[owner] = rank + 1
        at = owner * pairs + rank
        meta_ref[0, at] = lens_ref[0, me * slots + i]
        meta_ref[1, at] = i
        return carry

    lax.fori_loop(0, slots, place, 0)


def reducer(groups, owners, dp, me, src, out, refs):
    first, first_sum, second, second_sum, twin, twin_sum, third, mine = refs[:8]
    core_sems, pair_sems, twin_sems, row_sems, all_sems = refs[8:]
    sides = groups // 2
    core, side = lax.rem(dp, 2), dp // 2
    partner = side * 2 + (1 - core)

    def remote(source, target, sems, i, j, device):
        return pltpu.make_async_remote_copy(
            src_ref=source,
            dst_ref=target,
            send_sem=sems.at[0, i],
            recv_sem=sems.at[1, j],
            device_id=device,
            device_id_type=MESH,
        )

    wave = owners // 2

    def wave_of(h):
        return pl.ds(h * wave, wave)

    def swap(h):
        return remote(
            src.at[wave_of(h), 1 - core], first.at[wave_of(h)], core_sems, h, h, (partner, me)
        )

    def to_side(h, n, arriving):
        other = lax.rem(side + (sides - n if arriving else n), sides)
        slot = other if arriving else side
        target = lax.rem(side + n, sides)
        return remote(
            first_sum.at[target, wave_of(h)], second.at[slot, wave_of(h)], pair_sems,
            h * sides + n, h * sides + n, (target * 2 + core, me),
        )

    near = lax.rem(me, 2)
    mate = me + 1 - 2 * near
    pairs = owners // 2

    def pair_of(i):
        return lax.rem(me // 2 + 1 + i, pairs)

    def to_mate():
        return remote(second_sum.at[:, 1 - near], twin, twin_sems, 0, 0, (dp, mate))

    def to_owner(i, arriving):
        pair = lax.rem(me // 2 + i, pairs)
        slot = pair if arriving else me // 2
        return remote(
            twin_sum.at[pair], third.at[slot], row_sems, i, slot, (dp, pair * 2 + near)
        )

    def to_group(i, arriving):
        other = lax.rem(dp + i, groups)
        device = other if arriving else dp
        slot = lax.rem(device, 2) * sides + device // 2
        return remote(mine, out.at[slot], all_sems, i, slot, (other, me))

    def loop(low, high, body):
        def step(i, carry):
            body(i)
            return carry

        lax.fori_loop(low, high, step, 0)

    def stage_swap():
        for h in range(2):
            swap(h).start()

    def add_first(i):
        total = src[i, core].astype(F32) + first[i].astype(F32)
        for n in range(sides):
            first_sum[n, i] = total[n].astype(BF16)

    def stage_side():
        for h in range(2):
            swap(h).wait_recv()
            loop(h * wave, (h + 1) * wave, add_first)
            for n in range(1, sides):
                to_side(h, n, False).start()

    def add_second(i):
        for half in range(2):
            bucket = i * 2 + half
            total = first_sum[side, bucket].astype(F32)
            for n in range(1, sides):
                total = total + second[lax.rem(side + n, sides), bucket].astype(F32)
            second_sum[i, half] = total.astype(BF16)

    def stage_mate():
        for h in range(2):
            for n in range(1, sides):
                to_side(h, n, True).wait_recv()
        loop(0, pairs, add_second)
        to_mate().start()

    def add_twin(i):
        pair = pair_of(i)
        total = second_sum[pair, near].astype(F32) + twin[pair].astype(F32)
        twin_sum[pair] = total.astype(BF16)

    def twin_and_send(i):
        add_twin(i)
        to_owner(i + 1, False).start()

    def stage_owner():
        to_mate().wait_recv()
        loop(0, pairs - 1, twin_and_send)
        add_twin(pairs - 1)
        third[me // 2] = twin_sum[me // 2]

    def stage_group():
        loop(1, pairs, lambda i: to_owner(i, True).wait_recv())
        total = lax.fori_loop(
            1, pairs, lambda i, t: t + third[i].astype(F32), third[0].astype(F32)
        )
        mine[...] = total.astype(BF16)
        loop(1, groups, lambda i: to_group(i, False).start())
        out[core * sides + side] = mine[...]

    def stage_end():
        loop(1, groups, lambda i: to_group(i, True).wait_recv())

        for h in range(2):
            swap(h).wait_send()
            for n in range(1, sides):
                to_side(h, n, False).wait_send()
        to_mate().wait_send()
        loop(1, pairs, lambda i: to_owner(i, False).wait_send())
        loop(1, groups, lambda i: to_group(i, False).wait_send())

    return stage_swap, stage_side, stage_mate, stage_owner, stage_group, stage_end


def step_kernel(
    groups, owners, group, taps, size, early, early_out, bounds, total_frames,
    meta, *refs,
):
    sources, refs = refs[:12], refs[12:]
    grads_ref, arrived_ref, reduced_ref, reduced_out_ref, back_ref, ln_ref = refs[:6]
    targets, refs = refs[6:18], refs[18:]
    up, w_dw_ref, spec_ref, frames, w_in_ref, gain_ref, fwd_ref, inv_ref = targets[:8]
    w_out_ref, bn_gain_ref, bn_bias_ref, corr_ref = targets[8:]
    (
    stage, outgoing, arrive, outbuf,
    normed_s, inverse_s, linear_s, gate_s, h_s, spect_s, conv_s, fac_s, sw_s, dy_s, ga_s,
    w_taps, wspec, acc, xacc, tot, parts, mids, slots_a, slots_b, flat,
    packed, packed_out, local_sems, up_send, up_recv, out_send, out_recv,
    a_send, a_recv, b_send, b_recv, *reduce_refs,
    ) = refs
    dp, me = lax.axis_index("dp"), lax.axis_index("bucket")
    slot_count, span, width = frames.shape
    all_rows = slot_count * span
    own_rows = up.shape[0]
    blocks = width // LANES
    wide = w_in_ref.shape[1] // LANES
    chunk = all_rows // owners
    pairs = slot_count // owners
    steps = slot_count // group
    held = group // pairs
    grows = group * span
    half = size // 2
    far = owners // 2
    barrier = pltpu.get_barrier_semaphore()

    def loop(low, high, body):
        def step(i, carry):
            body(i)
            return carry

        lax.fori_loop(low, high, step, 0)

    def peer_of(m):
        bits = range((owners - 1).bit_length())
        return sum(lax.rem(me // 2**k + m // 2**k, 2) * 2**k for k in bits)

    def greet_group(i):
        pl.semaphore_signal(
            barrier, inc=1, device_id=(lax.rem(dp + i, groups), me), device_id_type=MESH
        )

    def greet_owner(m):
        pl.semaphore_signal(barrier, inc=1, device_id=(dp, peer_of(m)), device_id_type=MESH)

    loop(1, groups, greet_group)
    loop(1, owners, greet_owner)
    loads = [
        pltpu.make_async_copy(source, target, local_sems.at[n])
        for n, (source, target) in enumerate(zip(sources, targets))
    ]
    for load in loads:
        load.start()

    loads[0].wait()
    for c in range(blocks):
        stage[c, :own_rows] = up[:, lane(c)].astype(F32)
        stage[c, own_rows:] = jnp.zeros((chunk, LANES), F32)

    def lay_out(b):
        start = meta[2, b]
        for c in range(blocks):
            outgoing[b, :, lane(c)] = stage[c, pl.ds(start, chunk)].astype(BF16)

    loop(0, owners, lay_out)
    arrive[me] = outgoing[me]

    def sized(index, body):
        for rows in sorted(set(bounds)):
            low = bounds.index(rows)
            high = low + bounds.count(rows)

            @pl.when(jnp.logical_and(index >= low, index < high))
            def _():
                body(rows)

    def up_copy(m, part, rows, arriving):
        peer = peer_of(m)
        slot = peer if arriving else me
        span_of = pl.ds(0, early) if part == 0 else pl.ds(early, rows - early)
        return pltpu.make_async_remote_copy(
            src_ref=outgoing.at[peer, span_of],
            dst_ref=arrive.at[slot, span_of],
            send_sem=up_send.at[part, m],
            recv_sem=up_recv.at[part, m],
            device_id=(dp, peer),
            device_id_type=MESH,
        )

    cuts = (0, early_out, chunk)

    def out_copy(m, part, rows, arriving):
        peer = peer_of(m)
        slot = peer if arriving else me
        low, high = cuts[part], min(cuts[part + 1], rows)
        return pltpu.make_async_remote_copy(
            src_ref=outbuf.at[peer, pl.ds(low, high - low)],
            dst_ref=arrived_ref.at[slot, pl.ds(low, high - low)],
            send_sem=out_send.at[part, m],
            recv_sem=out_recv.at[part, m],
            device_id=(dp, peer),
            device_id_type=MESH,
        )

    def each_out(loader, m, part, arriving, use):
        def body(rows):
            if rows > cuts[part]:
                use(out_copy(m, part, rows, arriving))

        sized(loader, body)

    def start_out(low, high, part):
        loop(
            low,
            high,
            lambda j: each_out(me, owners - 1 - j, part, False, lambda copy: copy.start()),
        )

    def start_up(part):
        def body(j):
            m = owners - 1 - j
            if part == 0:
                up_copy(m, 0, None, False).start()
            else:
                sized(peer_of(m), lambda rows: up_copy(m, 1, rows, False).start())

        loop(0, owners - 1, body)

    def a_copy(n, i, arriving):
        other = lax.rem(dp + i, groups)
        slot = lax.rem(dp + groups - i, groups) if arriving else dp
        return pltpu.make_async_remote_copy(
            src_ref=parts.at[n],
            dst_ref=slots_a.at[n, slot],
            send_sem=a_send.at[i],
            recv_sem=a_recv.at[n, i],
            device_id=(other, me),
            device_id_type=MESH,
        )

    def b_copy(n, m, arriving):
        peer = peer_of(m)
        slot = peer if arriving else me
        return pltpu.make_async_remote_copy(
            src_ref=mids.at[n],
            dst_ref=slots_b.at[n, slot],
            send_sem=b_send.at[m],
            recv_sem=b_recv.at[n, m],
            device_id=(dp, peer),
            device_id_type=MESH,
        )

    def sum_start(n):
        for k in range(2):
            row = jnp.sum(acc[k], axis=0, keepdims=True)
            for c in range(blocks):
                parts[n, k * blocks + c : k * blocks + c + 1] = row[:, lane(c)]
        loop(1, groups, lambda i: a_copy(n, i, False).start())
        slots_a[n, dp] = parts[n]

    def sum_middle(n):
        loop(1, groups, lambda i: a_copy(n, i, True).wait_recv())
        mids[n] = lax.fori_loop(1, groups, lambda i, t: t + slots_a[n, i], slots_a[n, 0])
        loop(0, owners - 1, lambda j: b_copy(n, owners - 1 - j, False).start())
        slots_b[n, me] = mids[n]

    def sum_finish(n):
        loop(1, owners, lambda m: b_copy(n, m, True).wait_recv())
        loop(1, groups, lambda i: a_copy(n, i, False).wait_send())
        loop(1, owners, lambda m: b_copy(n, m, False).wait_send())
        return lax.fori_loop(1, owners, lambda i, t: t + slots_b[n, i], slots_b[n, 0])

    loads[1].wait()
    loads[2].wait()
    w_taps[...] = jnp.zeros_like(w_taps)
    w_taps[:taps] = w_dw_ref[...]
    wspec[...] = matmul_exact(spec_ref[...], w_taps[...])
    acc[...] = jnp.zeros_like(acc)
    pl.semaphore_wait(barrier, groups + owners - 2)
    start_up(0)
    for load in loads[3:8]:
        load.wait()

    def rows_of(i):
        return pl.ds(pl.multiple_of(i * grows, PACK), grows)

    def spec_rows(i):
        return pl.ds(pl.multiple_of(i * group * size, PACK), group * size)

    def lengths_of(i):
        return [meta[0, i * group + u] for u in range(group)]

    def packing(lengths):
        column = lax.broadcasted_iota(jnp.int32, (1, grows), 1)
        target = jnp.full((1, grows), -1, jnp.int32)
        for u in range(group):
            first = (u // pairs) * chunk + sum(lengths[u - u % pairs : u], jnp.int32(0))
            at = column - u * span
            live = jnp.logical_and(at >= 0, at < lengths[u])
            target = jnp.where(live, at + first, target)
        row = lax.broadcasted_iota(jnp.int32, (grows, grows), 0)
        return jnp.where(row == target, 1.0, 0.0).astype(BF16)

    def forward(i):
        rows = rows_of(i)
        lengths = lengths_of(i)
        values = jnp.concatenate(
            [frames[meta[1, i * group + u]] for u in range(group)], axis=0
        ).astype(F32)
        centred = values - jnp.mean(values, axis=1, keepdims=True)
        inverse = lax.rsqrt(jnp.mean(centred * centred, axis=1, keepdims=True) + EPSILON)
        normed = centred * inverse
        h = (normed * gain_ref[...]).astype(BF16)
        projected = matmul(h, w_in_ref[...])
        linear, gate = projected[:, :width], jax.nn.sigmoid(projected[:, width:])
        normed_s[rows] = normed
        inverse_s[rows] = jnp.broadcast_to(inverse, (grows, LANES))
        linear_s[rows] = linear
        gate_s[rows] = gate
        h_s[rows] = h
        gated = keep_live(linear * gate, lengths, span).astype(BF16)
        spect = matmul(fwd_ref[...], gated)
        spect_s[spec_rows(i)] = spect
        wr, wi, wn = wspec[:half], wspec[half : 2 * half], wspec[2 * half :]
        mixed = []
        for u in range(group):
            re = spect[u * size : u * size + half]
            im = spect[u * size + half : (u + 1) * size]
            mixed.append((wr * re - wi * im).astype(BF16))
            mixed.append((wn * im + wi * re).astype(BF16))
        conv = matmul(inv_ref[...], jnp.concatenate(mixed, axis=0))
        conv_s[rows] = conv
        masked = keep_live(conv, lengths, span)
        acc[0] += fold_rows(masked)
        acc[1] += fold_rows(masked * masked)

    loop(0, steps, forward)
    sum_start(0)
    sum_middle(0)
    for load in loads[8:]:
        load.wait()
    tot[...] = sum_finish(0)
    start_up(1)
    centre = row_of(tot, 0, blocks) / total_frames
    variance = row_of(tot, blocks, blocks) / total_frames - centre * centre
    bn_inverse = lax.rsqrt(variance + EPSILON)
    acc[...] = jnp.zeros_like(acc)
    bn_gain, bn_bias = bn_gain_ref[...], bn_bias_ref[...]

    def swish(i):
        rows = rows_of(i)
        bn_normed = (conv_s[rows] - centre) * bn_inverse
        conv_s[rows] = bn_normed
        bn = bn_normed * bn_gain + bn_bias
        sig = jax.nn.sigmoid(bn)
        swished = (bn * sig).astype(BF16)
        sw_s[rows] = swished
        fac_s[rows] = sig * (1.0 + bn * (1.0 - sig))
        out = matmul(swished, w_out_ref[...]).astype(BF16)
        out = matmul(packing(lengths_of(i)), out).astype(BF16)
        for r in range(held):
            outbuf[i * held + r] = out[r * chunk : (r + 1) * chunk]

    loop(0, steps, swish)

    @pl.when(me >= far)
    def _():
        start_out(0, far, 0)

    def middle(t):
        m = lax.rem(owners - t * held, owners)
        i = peer_of(m) // held
        rows = rows_of(i)
        lengths = lengths_of(i)
        for r in range(held):
            owner = i * held + r
            bits = range((owners - 1).bit_length())
            gap = sum(lax.rem(me // 2**k + owner // 2**k, 2) * 2**k for k in bits)

            @pl.when(owner != me)
            def _():
                up_copy(gap, 0, None, True).wait_recv()
                sized(me, lambda rows: up_copy(gap, 1, rows, True).wait_recv())

        pieces = []
        position = lax.broadcasted_iota(jnp.int32, (chunk, width), 0)
        for r in range(held):
            total = sum(lengths[r * pairs : (r + 1) * pairs], jnp.int32(0))
            came = arrive[i * held + r].astype(F32)
            pieces.append(jnp.where(position < total, came, 0.0).astype(BF16))
        dy = matmul_tn(packing(lengths), jnp.concatenate(pieces, axis=0)).astype(BF16)
        dy_s[rows] = dy
        grad_bn = matmul_nt(dy, w_out_ref[...]) * fac_s[rows]
        fac_s[rows] = grad_bn
        acc[0] += fold_rows(grad_bn)
        acc[1] += fold_rows(grad_bn * conv_s[rows])

    loop(0, steps, middle)
    sum_start(1)
    sum_middle(1)

    arrived_ref[me] = outbuf[me]

    share = width // owners
    per, per_out = -(-wide // groups), -(-blocks // groups)
    piece = share // groups
    sides = groups // 2
    in_stages = reducer(groups, owners, dp, me, packed, reduced_ref, reduce_refs[:13])
    out_stages = reducer(groups, owners, dp, me, packed_out, reduced_out_ref, reduce_refs[13:])

    def put(target, count, j, section, block):
        q, r = section // count, section % count
        target[j, q // sides, q % sides, r * share : (r + 1) * share] = block.astype(BF16)

    if per_out * groups != blocks:
        packed_out[...] = jnp.zeros_like(packed_out)
    if per * groups != wide or packed.shape[3] != per * share + piece:
        packed[...] = jnp.zeros_like(packed)
    for c in range(blocks):
        grad = matmul_tn(sw_s[:, lane(c)], dy_s[...])
        for n in range(LANES // share):
            j = c * (LANES // share) + n
            for s in range(blocks):
                put(packed_out, per_out, j, s, grad[n * share : (n + 1) * share, lane(s)])
    out_stages[0]()
    back_ref[...] = sum_finish(1)

    @pl.when(me < far)
    def _():
        start_out(0, far, 0)

    start_out(0, far, 1)
    start_out(far, owners - 1, 0)
    start_out(far, owners - 1, 1)
    bias_mean = row_of(back_ref, 0, blocks) / total_frames
    gain_mean = row_of(back_ref, blocks, blocks) / total_frames
    scale = bn_gain * bn_inverse
    xacc[...] = jnp.zeros_like(xacc)

    def backward(i):
        rows = rows_of(i)
        lengths = lengths_of(i)
        grad_conv = scale * (fac_s[rows] - bias_mean - conv_s[rows] * gain_mean)
        grad_conv = keep_live(grad_conv, lengths, span).astype(BF16)
        spect = matmul(fwd_ref[...], grad_conv)
        saved = spect_s[spec_rows(i)]
        wr, wi, wn = wspec[:half], wspec[half : 2 * half], wspec[2 * half :]
        mixed, terms = [], [None] * 3
        for u in range(group):
            re = spect[u * size : u * size + half]
            im = spect[u * size + half : (u + 1) * size]
            sre = saved[u * size : u * size + half]
            sim = saved[u * size + half : (u + 1) * size]
            mixed.append((wr * re + wi * im).astype(BF16))
            mixed.append((wn * im - wi * re).astype(BF16))
            new = (re * sre, im * sim, re * sim - im * sre)
            terms = [b if a is None else a + b for a, b in zip(terms, new)]
        for n in range(3):
            xacc[n * half : (n + 1) * half] += terms[n]
        grad_gated = matmul(inv_ref[...], jnp.concatenate(mixed, axis=0))
        grad_gated = keep_live(grad_gated, lengths, span)
        gate = gate_s[rows]
        left = grad_gated * gate
        ga_s[rows, :width] = left.astype(BF16)
        ga_s[rows, width:] = (left * linear_s[rows] * (1.0 - gate)).astype(BF16)

    loop(0, steps // 2, backward)
    out_stages[1]()
    loop(steps // 2, steps, backward)
    out_stages[2]()
    grad_taps = matmul_exact(corr_ref[...], xacc[...])
    flat[...] = jnp.zeros_like(flat)
    for c in range(blocks):
        grad = matmul_tn(h_s[:, lane(c)], ga_s[...])
        flat[: taps + 1] = grad_taps[:, lane(c)]
        turned = flat[...].T.astype(BF16)
        for n in range(LANES // share):
            j = c * (LANES // share) + n
            for s in range(wide):
                put(packed, per, j, s, grad[n * share : (n + 1) * share, lane(s)])
            for q in range(groups):
                packed[j, q // sides, q % sides, per * share : per * share + piece] = turned[
                    n * share + q * piece : n * share + (q + 1) * piece
                ]
    in_stages[0]()
    acc[...] = jnp.zeros_like(acc)

    def last(i):
        rows = rows_of(i)
        lengths = lengths_of(i)
        grad_h = matmul_nt(ga_s[rows], w_in_ref[...])
        normed, inverse = normed_s[rows], inverse_s[rows][:, :1]
        acc[0] += fold_rows(grad_h * normed)
        scaled = grad_h * gain_ref[...]
        inner_mean = jnp.mean(scaled * normed, axis=1, keepdims=True)
        grad_x = inverse * (scaled - jnp.mean(scaled, axis=1, keepdims=True) - normed * inner_mean)
        grads_ref[rows] = keep_live(grad_x, lengths, span).astype(BF16)

    loop(0, steps // 4, last)
    in_stages[1]()
    out_stages[3]()
    loop(steps // 4, steps, last)
    sum_start(2)
    in_stages[2]()
    sum_middle(2)
    in_stages[3]()
    out_stages[4]()
    in_stages[4]()
    ln_ref[...] = sum_finish(2)
    in_stages[5]()
    out_stages[5]()

    def finish_copies(m):
        up_copy(m, 0, None, False).wait_send()
        sized(peer_of(m), lambda rows: up_copy(m, 1, rows, False).wait_send())
        for part in range(2):
            each_out(peer_of(m), m, part, True, lambda copy: copy.wait_recv())
            each_out(me, m, part, False, lambda copy: copy.wait_send())
    loop(1, owners, finish_copies)


def finish_kernel(
    taps, per, per_out, piece, bounds,
    meta, grads_ref, arrived_ref, reduced_ref, reduced_out_ref, back_ref, ln_ref,
    out_ref, grad_frames_ref, win_ref, wout_ref, taps_ref, ln_out_ref, gain_ref, bias_ref,
    stage, flat, sems,
):
    me = lax.axis_index("bucket")
    owners, chunk, width = arrived_ref.shape
    own_rows = out_ref.shape[0]
    blocks = width // LANES
    share = win_ref.shape[0]
    wide = win_ref.shape[1] // LANES
    slots = sems.shape[0]
    span = grads_ref.shape[0] // slots

    def row_copy(i):
        source = pl.ds(pl.multiple_of(i * span, PACK), span)
        target = pl.ds(pl.multiple_of(meta[1, i] * span, PACK), span)
        return pltpu.make_async_copy(
            grads_ref.at[source], grad_frames_ref.at[target], sems.at[i]
        )

    def start(i, carry):
        row_copy(i).start()
        return carry

    lax.fori_loop(0, slots, start, 0)
    for b in range(owners):
        begin = meta[2, b]
        for c in range(blocks):
            stage[c, pl.ds(begin, bounds[b])] = arrived_ref[b, : bounds[b], lane(c)].astype(F32)
    for c in range(blocks):
        out_ref[:, lane(c)] = stage[c, :own_rows].astype(BF16)

    def section(source, count, s):
        q, r = s // count, s % count
        return source[q, r * share : (r + 1) * share].astype(F32)

    for c in range(blocks):
        wout_ref[:, lane(c)] = section(reduced_out_ref, per_out, c)
    for c in range(wide):
        win_ref[:, lane(c)] = section(reduced_ref, per, c)
    flat[...] = jnp.zeros_like(flat)
    for q in range(reduced_ref.shape[0]):
        flat[q * piece : (q + 1) * piece] = reduced_ref[
            q, per * share : per * share + piece
        ].astype(F32)
    taps_ref[...] = flat[...].T[:taps, :share]
    row = jnp.zeros((1, share), F32)
    for j in range(owners):
        c, n = j * share // LANES, j * share % LANES
        row = jnp.where(me == j, ln_ref[c : c + 1, n : n + share], row)
    ln_out_ref[...] = row
    bias_ref[...] = row_of(back_ref, 0, blocks)
    gain_ref[...] = row_of(back_ref, blocks, blocks)

    def wait(i, carry):
        row_copy(i).wait()
        return carry

    lax.fori_loop(0, slots, wait, 0)


def in_hbm(array):
    return pltpu.with_memory_space_constraint(array, pltpu.HBM)


def local(frames, lengths, owner_ids, upstream, ln_gain, w_in, w_dw, bn_gain, bn_bias, w_out):
    groups, owners = lax.axis_size("dp"), lax.axis_size("bucket")
    all_rows, width = frames.shape
    taps = w_dw.shape[1]
    slots = lengths.shape[1] // owners
    span = all_rows // slots
    pairs = slots // owners
    own_rows = upstream.shape[0]
    blocks = width // LANES
    wide = w_in.shape[1] // LANES
    total_frames = float(own_rows * owners * groups)
    in_vmem = pl.BlockSpec(memory_space=pltpu.VMEM)
    in_smem = pl.BlockSpec(memory_space=pltpu.SMEM)
    anywhere = pl.BlockSpec(memory_space=pl.ANY)
    group = pairs * max(1, 4 // pairs)
    size, fwd, inv, spec, corr = transform_tables(span, taps, group)
    chunk = pairs * span
    bounds = chunk_bounds(own_rows, pairs, span, owners)
    early = max(PACK, min(chunk // 2 // PACK * PACK, bounds[0] - PACK))
    early_out = max(PACK, min(chunk * 5 // 12 // PACK * PACK, bounds[0] - PACK))
    share = width // owners
    per, per_out = -(-wide // groups), -(-blocks // groups)
    piece = share // groups
    sides = groups // 2
    rows_in = (per * share + -(-piece // PACK) * PACK, LANES)
    rows_out = (per_out * share, LANES)

    meta = pl.pallas_call(
        functools.partial(tables_kernel, slots),
        in_specs=[in_smem, in_smem],
        out_specs=in_smem,
        out_shape=jax.ShapeDtypeStruct((3, slots), jnp.int32),
        scratch_shapes=[pltpu.SMEM((owners,), jnp.int32)],
        compiler_params=pltpu.CompilerParams(vmem_limit_bytes=1 << 20),
        name="tables",
    )(in_hbm(lengths), in_hbm(owner_ids))

    operands = (
        upstream, w_dw.T, spec, frames.reshape(slots, span, width), w_in, ln_gain[None], fwd, inv,
        w_out, bn_gain[None], bn_bias[None], corr,
    )
    sums_shape = (2 * blocks, LANES)
    tall = pltpu.VMEM((all_rows, width), F32)
    short = pltpu.VMEM((all_rows, width), BF16)
    chunks = pltpu.VMEM((owners, chunk, width), BF16)

    def reduce_scratch(kind):
        return [
            pltpu.VMEM((owners, sides) + kind, BF16),
            pltpu.VMEM((sides, owners) + kind, BF16),
            pltpu.VMEM((sides, owners) + kind, BF16),
            pltpu.VMEM((owners // 2, 2) + kind, BF16),
            pltpu.VMEM((owners // 2,) + kind, BF16),
            pltpu.VMEM((owners // 2,) + kind, BF16),
            pltpu.VMEM((owners // 2,) + kind, BF16),
            pltpu.VMEM(kind, BF16),
            pltpu.SemaphoreType.DMA((2, 2)),
            pltpu.SemaphoreType.DMA((2, 2 * sides)),
            pltpu.SemaphoreType.DMA((2, 1)),
            pltpu.SemaphoreType.DMA((2, owners // 2)),
            pltpu.SemaphoreType.DMA((2, groups)),
        ]

    grads, arrived, reduced, reduced_out, back, ln_total = pl.pallas_call(
        functools.partial(
            step_kernel,
            groups, owners, group, taps, size, early, early_out, bounds,
            total_frames,
        ),
        in_specs=[in_smem] + [anywhere] * 12,
        out_specs=[in_vmem] * 6,
        out_shape=[
            jax.ShapeDtypeStruct((all_rows, width), BF16),
            jax.ShapeDtypeStruct((owners, chunk, width), BF16),
            jax.ShapeDtypeStruct((groups,) + rows_in, BF16),
            jax.ShapeDtypeStruct((groups,) + rows_out, BF16),
            jax.ShapeDtypeStruct(sums_shape, F32),
            jax.ShapeDtypeStruct(sums_shape, F32),
        ],
        scratch_shapes=[pltpu.VMEM(operand.shape, operand.dtype) for operand in operands]
        + [
            pltpu.VMEM((blocks, own_rows + chunk, LANES), F32),
            chunks,
            chunks,
            chunks,
            tall,
            pltpu.VMEM((all_rows, LANES), F32),
            tall,
            tall,
            short,
            pltpu.VMEM((slots * size, width), F32),
            tall,
            tall,
            short,
            short,
            pltpu.VMEM((all_rows, w_in.shape[1]), BF16),
            pltpu.VMEM((taps + 1, width), F32),
            pltpu.VMEM((3 * size // 2, width), F32),
            pltpu.VMEM((2, SUB, width), F32),
            pltpu.VMEM((3 * size // 2, width), F32),
            pltpu.VMEM(sums_shape, F32),
            pltpu.VMEM((3,) + sums_shape, F32),
            pltpu.VMEM((3,) + sums_shape, F32),
            pltpu.VMEM((3, groups) + sums_shape, F32),
            pltpu.VMEM((3, owners) + sums_shape, F32),
            pltpu.VMEM((LANES, LANES), F32),
            pltpu.VMEM((owners, 2, sides) + rows_in, BF16),
            pltpu.VMEM((owners, 2, sides) + rows_out, BF16),
            pltpu.SemaphoreType.DMA((12,)),
            pltpu.SemaphoreType.DMA((2, owners)),
            pltpu.SemaphoreType.DMA((2, owners)),
            pltpu.SemaphoreType.DMA((2, owners)),
            pltpu.SemaphoreType.DMA((2, owners)),
            pltpu.SemaphoreType.DMA((groups,)),
            pltpu.SemaphoreType.DMA((3, groups)),
            pltpu.SemaphoreType.DMA((owners,)),
            pltpu.SemaphoreType.DMA((3, owners)),
        ]
        + reduce_scratch(rows_in)
        + reduce_scratch(rows_out),
        compiler_params=pltpu.CompilerParams(
            collective_id=0, has_side_effects=True, vmem_limit_bytes=STEP_VMEM
        ),
        cost_estimate=pl.CostEstimate(
            flops=10**10, bytes_accessed=4 * 10**7, transcendentals=0
        ),
        name="step",
    )(meta, *map(in_hbm, operands))

    row_shape = jax.ShapeDtypeStruct((1, width), F32)
    out_frames, grad_frames, grad_win, grad_wo, grad_taps, grad_ln, grad_gain, grad_bias = (
        pl.pallas_call(
            functools.partial(finish_kernel, taps, per, per_out, piece, bounds),
            in_specs=[in_smem] + [in_vmem] * 6,
            out_specs=[in_vmem, anywhere] + [in_vmem] * 6,
            out_shape=[
                jax.ShapeDtypeStruct((own_rows, width), BF16),
                jax.ShapeDtypeStruct((all_rows, width), BF16),
                jax.ShapeDtypeStruct((share, w_in.shape[1]), F32),
                jax.ShapeDtypeStruct((share, width), F32),
                jax.ShapeDtypeStruct((taps, share), F32),
                jax.ShapeDtypeStruct((1, share), F32),
                row_shape,
                row_shape,
            ],
            scratch_shapes=[
                pltpu.VMEM((blocks, own_rows + chunk, LANES), F32),
                pltpu.VMEM((LANES, LANES), F32),
                pltpu.SemaphoreType.DMA((slots,)),
            ],
            compiler_params=pltpu.CompilerParams(vmem_limit_bytes=8 << 20),
            name="finish",
        )(meta, grads, arrived, reduced, reduced_out, back, ln_total)
    )
    return (
        out_frames,
        grad_frames,
        grad_win,
        grad_wo,
        grad_taps.T,
        grad_ln[0],
        grad_gain[0],
        grad_bias[0],
    )


def solution(mesh):
    placed = (
        P(("dp", "bucket"), None),
        P("dp", None),
        P("dp", None),
        P(("dp", "bucket"), None),
        P(),
        P(),
        P(),
        P(),
        P(),
        P(),
    )
    return jax.shard_map(
        local,
        mesh=mesh,
        in_specs=placed,
        out_specs=(
            P(("dp", "bucket"), None),
            P(("dp", "bucket"), None),
            P("bucket", None),
            P("bucket", None),
            P("bucket", None),
            P("bucket"),
            P(),
            P(),
        ),
        check_vma=False,
    )
```

```python
import functools

import jax
import jax.numpy as jnp
import numpy as np
from jax import lax
from jax.experimental import pallas as pl
from jax.experimental.pallas import tpu as pltpu
from jax.sharding import PartitionSpec as P

EPSILON = 1e-05
LANES = 128
SUB = 8
PACK = 16
STEP_VMEM = 50 << 20
MESH = pl.DeviceIdType.MESH
BF16 = jnp.bfloat16
F32 = jnp.float32


def lane(c):
    return slice(c * LANES, (c + 1) * LANES)


def row_of(packed, first, blocks):
    return jnp.concatenate([packed[first + c : first + c + 1] for c in range(blocks)], axis=1)


def keep_live(values, lengths, span):
    position = lax.broadcasted_iota(jnp.int32, (span, values.shape[1]), 0)
    parts = [
        jnp.where(position < length, values[i * span : (i + 1) * span], 0.0)
        for i, length in enumerate(lengths)
    ]
    return jnp.concatenate(parts, axis=0)


def fold_rows(values):
    rows, width = values.shape
    return jnp.sum(values.reshape(rows // SUB, SUB, width), axis=0)


def matmul(a, b):
    return jnp.dot(a, b, preferred_element_type=F32)


def matmul_nt(a, b):
    return lax.dot_general(a, b, (((1,), (1,)), ((), ())), preferred_element_type=F32)


def matmul_tn(a, b):
    return lax.dot_general(a, b, (((0,), (0,)), ((), ())), preferred_element_type=F32)


def matmul_exact(a, b):
    return jnp.dot(a, b, preferred_element_type=F32, precision=lax.Precision.HIGHEST)


def transform_tables(span, taps, group):
    size = -(-(span + taps // 2) // (2 * PACK)) * (2 * PACK)
    half = size // 2
    freq = np.arange(half)[:, None]

    def angle(times):
        return 2.0 * np.pi * freq * np.asarray(times)[None, :] / size

    def flip(times):
        return np.where(np.asarray(times) % 2 == 0, 1.0, -1.0)

    times = np.arange(span)
    real, imag = np.cos(angle(times)), -np.sin(angle(times))
    imag[0] = flip(times)
    forward = np.concatenate([real, imag], axis=0)
    scale = np.where(np.arange(size) % half == 0, 1.0, 2.0) / size
    inverse = (forward * scale[:, None]).T
    lags = taps // 2 - np.arange(taps)
    wr, wi, wn = np.cos(angle(lags)), -np.sin(angle(lags)), np.cos(angle(lags))
    wi[0] = 0.0
    wn[0] = flip(lags)
    spectrum = np.concatenate([wr, wi, wn], axis=0)
    spectrum = np.pad(spectrum, ((0, 0), (0, 1)))
    back = -lags
    cr, cn, ci = np.cos(angle(back)), np.cos(angle(back)), -np.sin(angle(back))
    cn[0] = flip(back)
    ci[0] = 0.0
    both = np.concatenate([scale[:half], scale[half:], scale[half:]])
    correlate = (np.concatenate([cr, cn, ci], axis=0) * both[:, None]).T
    correlate = np.pad(correlate, ((0, 1), (0, 0)))
    eye = np.eye(group)
    return (
        size,
        jnp.asarray(np.kron(eye, forward), BF16),
        jnp.asarray(np.kron(eye, inverse), BF16),
        jnp.asarray(spectrum, F32),
        jnp.asarray(correlate, F32),
    )


def chunk_bounds(own_rows, pairs, span, loaders):
    rows = [min(pairs * span, (own_rows - b * pairs) // (loaders - b)) for b in range(loaders)]
    return [-(-r // PACK) * PACK for r in rows]


def tables_kernel(slots, lens_ref, owners_ref, meta_ref, counts):
    me = lax.axis_index("bucket")
    loaders = lens_ref.shape[1] // slots
    pairs = slots // loaders

    def look(b, start):
        meta_ref[2, b] = start
        for j in range(slots):
            at = b * slots + j
            start = start + jnp.where(owners_ref[0, at] == me, lens_ref[0, at], 0)
        return start

    lax.fori_loop(0, loaders, look, jnp.int32(0))

    def clear(i, carry):
        counts[i] = 0
        return carry

    lax.fori_loop(0, loaders, clear, 0)

    def place(i, carry):
        owner = owners_ref[0, me * slots + i]
        rank = counts[owner]
        counts[owner] = rank + 1
        at = owner * pairs + rank
        meta_ref[0, at] = lens_ref[0, me * slots + i]
        meta_ref[1, at] = i
        return carry

    lax.fori_loop(0, slots, place, 0)


def reducer(groups, owners, dp, me, src, out, refs):
    first, first_sum, second, second_sum, twin, twin_sum, third, mine = refs[:8]
    core_sems, pair_sems, twin_sems, row_sems, all_sems = refs[8:]
    sides = groups // 2
    core, side = lax.rem(dp, 2), dp // 2
    partner = side * 2 + (1 - core)

    def remote(source, target, sems, i, j, device):
        return pltpu.make_async_remote_copy(
            src_ref=source,
            dst_ref=target,
            send_sem=sems.at[0, i],
            recv_sem=sems.at[1, j],
            device_id=device,
            device_id_type=MESH,
        )

    wave = owners // 2

    def wave_of(h):
        return pl.ds(h * wave, wave)

    def swap(h):
        return remote(
            src.at[wave_of(h), 1 - core], first.at[wave_of(h)], core_sems, h, h, (partner, me)
        )

    def to_side(h, n, arriving):
        other = lax.rem(side + (sides - n if arriving else n), sides)
        slot = other if arriving else side
        target = lax.rem(side + n, sides)
        return remote(
            first_sum.at[target, wave_of(h)], second.at[slot, wave_of(h)], pair_sems,
            h * sides + n, h * sides + n, (target * 2 + core, me),
        )

    near = lax.rem(me, 2)
    mate = me + 1 - 2 * near
    pairs = owners // 2

    def pair_of(i):
        return lax.rem(me // 2 + 1 + i, pairs)

    def to_mate():
        return remote(second_sum.at[:, 1 - near], twin, twin_sems, 0, 0, (dp, mate))

    def to_owner(i, arriving):
        pair = lax.rem(me // 2 + i, pairs)
        slot = pair if arriving else me // 2
        return remote(
            twin_sum.at[pair], third.at[slot], row_sems, i, slot, (dp, pair * 2 + near)
        )

    def to_group(i, arriving):
        other = lax.rem(dp + i, groups)
        device = other if arriving else dp
        slot = lax.rem(device, 2) * sides + device // 2
        return remote(mine, out.at[slot], all_sems, i, slot, (other, me))

    def loop(low, high, body):
        def step(i, carry):
            body(i)
            return carry

        lax.fori_loop(low, high, step, 0)

    def stage_swap(h):
        swap(h).start()

    def add_first(i):
        total = src[i, core].astype(F32) + first[i].astype(F32)
        for n in range(sides):
            first_sum[n, i] = total[n].astype(BF16)

    def stage_side():
        for h in range(2):
            swap(h).wait_recv()
            loop(h * wave, (h + 1) * wave, add_first)
            for n in range(1, sides):
                to_side(h, n, False).start()

    def add_second(i):
        for half in range(2):
            bucket = i * 2 + half
            total = first_sum[side, bucket].astype(F32)
            for n in range(1, sides):
                total = total + second[lax.rem(side + n, sides), bucket].astype(F32)
            second_sum[i, half] = total.astype(BF16)

    def stage_mate():
        for h in range(2):
            for n in range(1, sides):
                to_side(h, n, True).wait_recv()
        loop(0, pairs, add_second)
        to_mate().start()

    def add_twin(i):
        pair = pair_of(i)
        total = second_sum[pair, near].astype(F32) + twin[pair].astype(F32)
        twin_sum[pair] = total.astype(BF16)

    def twin_and_send(i):
        add_twin(i)
        to_owner(i + 1, False).start()

    def stage_owner():
        to_mate().wait_recv()
        loop(0, pairs - 1, twin_and_send)
        add_twin(pairs - 1)
        third[me // 2] = twin_sum[me // 2]

    def stage_group():
        loop(1, pairs, lambda i: to_owner(i, True).wait_recv())
        total = lax.fori_loop(
            1, pairs, lambda i, t: t + third[i].astype(F32), third[0].astype(F32)
        )
        mine[...] = total.astype(BF16)
        loop(1, groups, lambda i: to_group(i, False).start())
        out[core * sides + side] = mine[...]

    def stage_end():
        loop(1, groups, lambda i: to_group(i, True).wait_recv())

        for h in range(2):
            swap(h).wait_send()
            for n in range(1, sides):
                to_side(h, n, False).wait_send()
        to_mate().wait_send()
        loop(1, pairs, lambda i: to_owner(i, False).wait_send())
        loop(1, groups, lambda i: to_group(i, False).wait_send())

    return stage_swap, stage_side, stage_mate, stage_owner, stage_group, stage_end


def step_kernel(
    groups, owners, group, taps, size, early, early_out, bounds, total_frames,
    meta, *refs,
):
    sources, refs = refs[:12], refs[12:]
    grads_ref, arrived_ref, reduced_ref, reduced_out_ref, back_ref, ln_ref = refs[:6]
    targets, refs = refs[6:18], refs[18:]
    up, w_dw_ref, spec_ref, frames, w_in_ref, gain_ref, fwd_ref, inv_ref = targets[:8]
    w_out_ref, bn_gain_ref, bn_bias_ref, corr_ref = targets[8:]
    (
    stage, outgoing, arrive, outbuf,
    normed_s, inverse_s, linear_s, gate_s, h_s, spect_s, conv_s, fac_s, sw_s, dy_s, ga_s,
    w_taps, wspec, acc, xacc, tot, parts, mids, slots_a, slots_b, flat,
    packed, packed_out, local_sems, up_send, up_recv, out_send, out_recv,
    a_send, a_recv, b_send, b_recv, *reduce_refs,
    ) = refs
    dp, me = lax.axis_index("dp"), lax.axis_index("bucket")
    slot_count, span, width = frames.shape
    all_rows = slot_count * span
    own_rows = up.shape[0]
    blocks = width // LANES
    wide = w_in_ref.shape[1] // LANES
    chunk = all_rows // owners
    pairs = slot_count // owners
    steps = slot_count // group
    held = group // pairs
    grows = group * span
    half = size // 2
    far = owners // 2
    barrier = pltpu.get_barrier_semaphore()

    def loop(low, high, body):
        def step(i, carry):
            body(i)
            return carry

        lax.fori_loop(low, high, step, 0)

    def peer_of(m):
        bits = range((owners - 1).bit_length())
        return sum(lax.rem(me // 2**k + m // 2**k, 2) * 2**k for k in bits)

    def greet_group(i):
        pl.semaphore_signal(
            barrier, inc=1, device_id=(lax.rem(dp + i, groups), me), device_id_type=MESH
        )

    def greet_owner(m):
        pl.semaphore_signal(barrier, inc=1, device_id=(dp, peer_of(m)), device_id_type=MESH)

    loop(1, groups, greet_group)
    loop(1, owners, greet_owner)
    loads = [
        pltpu.make_async_copy(source, target, local_sems.at[n])
        for n, (source, target) in enumerate(zip(sources, targets))
    ]
    for load in loads:
        load.start()

    loads[0].wait()
    for c in range(blocks):
        stage[c, :own_rows] = up[:, lane(c)].astype(F32)
        stage[c, own_rows:] = jnp.zeros((chunk, LANES), F32)

    def lay_out(b):
        start = meta[2, b]
        for c in range(blocks):
            outgoing[b, :, lane(c)] = stage[c, pl.ds(start, chunk)].astype(BF16)

    loop(0, owners, lay_out)
    arrive[me] = outgoing[me]

    def sized(index, body):
        for rows in sorted(set(bounds)):
            low = bounds.index(rows)
            high = low + bounds.count(rows)

            @pl.when(jnp.logical_and(index >= low, index < high))
            def _():
                body(rows)

    def up_copy(m, part, rows, arriving):
        peer = peer_of(m)
        slot = peer if arriving else me
        span_of = pl.ds(0, early) if part == 0 else pl.ds(early, rows - early)
        return pltpu.make_async_remote_copy(
            src_ref=outgoing.at[peer, span_of],
            dst_ref=arrive.at[slot, span_of],
            send_sem=up_send.at[part, m],
            recv_sem=up_recv.at[part, m],
            device_id=(dp, peer),
            device_id_type=MESH,
        )

    cuts = (0, early_out, chunk)

    def out_copy(m, part, rows, arriving):
        peer = peer_of(m)
        slot = peer if arriving else me
        low, high = cuts[part], min(cuts[part + 1], rows)
        return pltpu.make_async_remote_copy(
            src_ref=outbuf.at[peer, pl.ds(low, high - low)],
            dst_ref=arrived_ref.at[slot, pl.ds(low, high - low)],
            send_sem=out_send.at[part, m],
            recv_sem=out_recv.at[part, m],
            device_id=(dp, peer),
            device_id_type=MESH,
        )

    def each_out(loader, m, part, arriving, use):
        def body(rows):
            if rows > cuts[part]:
                use(out_copy(m, part, rows, arriving))

        sized(loader, body)

    def start_out(low, high, part):
        loop(
            low,
            high,
            lambda j: each_out(me, owners - 1 - j, part, False, lambda copy: copy.start()),
        )

    def start_up(part):
        def body(j):
            m = owners - 1 - j
            if part == 0:
                up_copy(m, 0, None, False).start()
            else:
                sized(peer_of(m), lambda rows: up_copy(m, 1, rows, False).start())

        loop(0, owners - 1, body)

    def a_copy(n, i, arriving):
        other = lax.rem(dp + i, groups)
        slot = lax.rem(dp + groups - i, groups) if arriving else dp
        return pltpu.make_async_remote_copy(
            src_ref=parts.at[n],
            dst_ref=slots_a.at[n, slot],
            send_sem=a_send.at[i],
            recv_sem=a_recv.at[n, i],
            device_id=(other, me),
            device_id_type=MESH,
        )

    def b_copy(n, m, arriving):
        peer = peer_of(m)
        slot = peer if arriving else me
        return pltpu.make_async_remote_copy(
            src_ref=mids.at[n],
            dst_ref=slots_b.at[n, slot],
            send_sem=b_send.at[m],
            recv_sem=b_recv.at[n, m],
            device_id=(dp, peer),
            device_id_type=MESH,
        )

    def sum_start(n):
        for k in range(2):
            row = jnp.sum(acc[k], axis=0, keepdims=True)
            for c in range(blocks):
                parts[n, k * blocks + c : k * blocks + c + 1] = row[:, lane(c)]
        loop(1, groups, lambda i: a_copy(n, i, False).start())
        slots_a[n, dp] = parts[n]

    def sum_middle(n):
        loop(1, groups, lambda i: a_copy(n, i, True).wait_recv())
        mids[n] = lax.fori_loop(1, groups, lambda i, t: t + slots_a[n, i], slots_a[n, 0])
        loop(0, owners - 1, lambda j: b_copy(n, owners - 1 - j, False).start())
        slots_b[n, me] = mids[n]

    def sum_finish(n):
        loop(1, owners, lambda m: b_copy(n, m, True).wait_recv())
        loop(1, groups, lambda i: a_copy(n, i, False).wait_send())
        loop(1, owners, lambda m: b_copy(n, m, False).wait_send())
        return lax.fori_loop(1, owners, lambda i, t: t + slots_b[n, i], slots_b[n, 0])

    loads[1].wait()
    loads[2].wait()
    w_taps[...] = jnp.zeros_like(w_taps)
    w_taps[:taps] = w_dw_ref[...]
    wspec[...] = matmul_exact(spec_ref[...], w_taps[...])
    acc[...] = jnp.zeros_like(acc)
    pl.semaphore_wait(barrier, groups + owners - 2)
    start_up(0)
    for load in loads[3:8]:
        load.wait()

    def rows_of(i):
        return pl.ds(pl.multiple_of(i * grows, PACK), grows)

    def spec_rows(i):
        return pl.ds(pl.multiple_of(i * group * size, PACK), group * size)

    def lengths_of(i):
        return [meta[0, i * group + u] for u in range(group)]

    def packing(lengths):
        column = lax.broadcasted_iota(jnp.int32, (1, grows), 1)
        target = jnp.full((1, grows), -1, jnp.int32)
        for u in range(group):
            first = (u // pairs) * chunk + sum(lengths[u - u % pairs : u], jnp.int32(0))
            at = column - u * span
            live = jnp.logical_and(at >= 0, at < lengths[u])
            target = jnp.where(live, at + first, target)
        row = lax.broadcasted_iota(jnp.int32, (grows, grows), 0)
        return jnp.where(row == target, 1.0, 0.0).astype(BF16)

    def forward(i):
        rows = rows_of(i)
        lengths = lengths_of(i)
        values = jnp.concatenate(
            [frames[meta[1, i * group + u]] for u in range(group)], axis=0
        ).astype(F32)
        centred = values - jnp.mean(values, axis=1, keepdims=True)
        inverse = lax.rsqrt(jnp.mean(centred * centred, axis=1, keepdims=True) + EPSILON)
        normed = centred * inverse
        h = (normed * gain_ref[...]).astype(BF16)
        projected = matmul(h, w_in_ref[...])
        linear, gate = projected[:, :width], jax.nn.sigmoid(projected[:, width:])
        normed_s[rows] = normed
        inverse_s[rows] = jnp.broadcast_to(inverse, (grows, LANES))
        linear_s[rows] = linear
        gate_s[rows] = gate
        h_s[rows] = h
        gated = keep_live(linear * gate, lengths, span).astype(BF16)
        spect = matmul(fwd_ref[...], gated)
        spect_s[spec_rows(i)] = spect
        wr, wi, wn = wspec[:half], wspec[half : 2 * half], wspec[2 * half :]
        mixed = []
        for u in range(group):
            re = spect[u * size : u * size + half]
            im = spect[u * size + half : (u + 1) * size]
            mixed.append((wr * re - wi * im).astype(BF16))
            mixed.append((wn * im + wi * re).astype(BF16))
        conv = matmul(inv_ref[...], jnp.concatenate(mixed, axis=0))
        conv_s[rows] = conv
        masked = keep_live(conv, lengths, span)
        acc[0] += fold_rows(masked)
        acc[1] += fold_rows(masked * masked)

    loop(0, steps, forward)
    sum_start(0)
    sum_middle(0)
    for load in loads[8:]:
        load.wait()
    tot[...] = sum_finish(0)
    start_up(1)
    centre = row_of(tot, 0, blocks) / total_frames
    variance = row_of(tot, blocks, blocks) / total_frames - centre * centre
    bn_inverse = lax.rsqrt(variance + EPSILON)
    acc[...] = jnp.zeros_like(acc)
    bn_gain, bn_bias = bn_gain_ref[...], bn_bias_ref[...]

    def swish(i):
        rows = rows_of(i)
        bn_normed = (conv_s[rows] - centre) * bn_inverse
        conv_s[rows] = bn_normed
        bn = bn_normed * bn_gain + bn_bias
        sig = jax.nn.sigmoid(bn)
        swished = (bn * sig).astype(BF16)
        sw_s[rows] = swished
        fac_s[rows] = sig * (1.0 + bn * (1.0 - sig))
        out = matmul(swished, w_out_ref[...]).astype(BF16)
        out = matmul(packing(lengths_of(i)), out).astype(BF16)
        for r in range(held):
            outbuf[i * held + r] = out[r * chunk : (r + 1) * chunk]

    loop(0, steps, swish)

    @pl.when(me >= far)
    def _():
        start_out(0, far, 0)

    def middle(t):
        m = lax.rem(owners - t * held, owners)
        i = peer_of(m) // held
        rows = rows_of(i)
        lengths = lengths_of(i)
        for r in range(held):
            owner = i * held + r
            bits = range((owners - 1).bit_length())
            gap = sum(lax.rem(me // 2**k + owner // 2**k, 2) * 2**k for k in bits)

            @pl.when(owner != me)
            def _():
                up_copy(gap, 0, None, True).wait_recv()
                sized(me, lambda rows: up_copy(gap, 1, rows, True).wait_recv())

        pieces = []
        position = lax.broadcasted_iota(jnp.int32, (chunk, width), 0)
        for r in range(held):
            total = sum(lengths[r * pairs : (r + 1) * pairs], jnp.int32(0))
            came = arrive[i * held + r].astype(F32)
            pieces.append(jnp.where(position < total, came, 0.0).astype(BF16))
        dy = matmul_tn(packing(lengths), jnp.concatenate(pieces, axis=0)).astype(BF16)
        dy_s[rows] = dy
        grad_bn = matmul_nt(dy, w_out_ref[...]) * fac_s[rows]
        fac_s[rows] = grad_bn
        acc[0] += fold_rows(grad_bn)
        acc[1] += fold_rows(grad_bn * conv_s[rows])

    loop(0, steps, middle)
    sum_start(1)
    sum_middle(1)

    arrived_ref[me] = outbuf[me]

    share = width // owners
    per, per_out = -(-wide // groups), -(-blocks // groups)
    piece = share // groups
    sides = groups // 2
    in_stages = reducer(groups, owners, dp, me, packed, reduced_ref, reduce_refs[:13])
    out_stages = reducer(groups, owners, dp, me, packed_out, reduced_out_ref, reduce_refs[13:])

    def put(target, count, j, section, block):
        q, r = section // count, section % count
        target[j, q // sides, q % sides, r * share : (r + 1) * share] = block.astype(BF16)

    if per_out * groups != blocks:
        packed_out[...] = jnp.zeros_like(packed_out)
    if per * groups != wide or packed.shape[3] != per * share + piece:
        packed[...] = jnp.zeros_like(packed)
    for c in range(blocks):
        grad = matmul_tn(sw_s[:, lane(c)], dy_s[...])
        for n in range(LANES // share):
            j = c * (LANES // share) + n
            for s in range(blocks):
                put(packed_out, per_out, j, s, grad[n * share : (n + 1) * share, lane(s)])
        if c % (blocks // 2) == blocks // 2 - 1:
            out_stages[0](c // (blocks // 2))
    back_ref[...] = sum_finish(1)

    @pl.when(me < far)
    def _():
        start_out(0, far, 0)

    start_out(0, far, 1)
    start_out(far, owners - 1, 0)
    start_out(far, owners - 1, 1)
    bias_mean = row_of(back_ref, 0, blocks) / total_frames
    gain_mean = row_of(back_ref, blocks, blocks) / total_frames
    scale = bn_gain * bn_inverse
    xacc[...] = jnp.zeros_like(xacc)

    def backward(i):
        rows = rows_of(i)
        lengths = lengths_of(i)
        grad_conv = scale * (fac_s[rows] - bias_mean - conv_s[rows] * gain_mean)
        grad_conv = keep_live(grad_conv, lengths, span).astype(BF16)
        spect = matmul(fwd_ref[...], grad_conv)
        saved = spect_s[spec_rows(i)]
        wr, wi, wn = wspec[:half], wspec[half : 2 * half], wspec[2 * half :]
        mixed, terms = [], [None] * 3
        for u in range(group):
            re = spect[u * size : u * size + half]
            im = spect[u * size + half : (u + 1) * size]
            sre = saved[u * size : u * size + half]
            sim = saved[u * size + half : (u + 1) * size]
            mixed.append((wr * re + wi * im).astype(BF16))
            mixed.append((wn * im - wi * re).astype(BF16))
            new = (re * sre, im * sim, re * sim - im * sre)
            terms = [b if a is None else a + b for a, b in zip(terms, new)]
        for n in range(3):
            xacc[n * half : (n + 1) * half] += terms[n]
        grad_gated = matmul(inv_ref[...], jnp.concatenate(mixed, axis=0))
        grad_gated = keep_live(grad_gated, lengths, span)
        gate = gate_s[rows]
        left = grad_gated * gate
        ga_s[rows, :width] = left.astype(BF16)
        ga_s[rows, width:] = (left * linear_s[rows] * (1.0 - gate)).astype(BF16)

    def twice(body):
        def both(i):
            body(2 * i)
            body(2 * i + 1)

        return both

    loop(0, steps // 4, twice(backward))
    out_stages[1]()
    loop(steps // 4, steps // 2, twice(backward))
    out_stages[2]()
    grad_taps = matmul_exact(corr_ref[...], xacc[...])
    flat[...] = jnp.zeros_like(flat)
    for c in range(blocks):
        grad = matmul_tn(h_s[:, lane(c)], ga_s[...])
        flat[: taps + 1] = grad_taps[:, lane(c)]
        turned = flat[...].T.astype(BF16)
        for n in range(LANES // share):
            j = c * (LANES // share) + n
            for s in range(wide):
                put(packed, per, j, s, grad[n * share : (n + 1) * share, lane(s)])
            for q in range(groups):
                packed[j, q // sides, q % sides, per * share : per * share + piece] = turned[
                    n * share + q * piece : n * share + (q + 1) * piece
                ]
        if c % (blocks // 2) == blocks // 2 - 1:
            in_stages[0](c // (blocks // 2))
    acc[...] = jnp.zeros_like(acc)

    def last(i):
        rows = rows_of(i)
        lengths = lengths_of(i)
        grad_h = matmul_nt(ga_s[rows], w_in_ref[...])
        normed, inverse = normed_s[rows], inverse_s[rows][:, :1]
        acc[0] += fold_rows(grad_h * normed)
        scaled = grad_h * gain_ref[...]
        inner_mean = jnp.mean(scaled * normed, axis=1, keepdims=True)
        grad_x = inverse * (scaled - jnp.mean(scaled, axis=1, keepdims=True) - normed * inner_mean)
        grads_ref[rows] = keep_live(grad_x, lengths, span).astype(BF16)

    loop(0, steps // 4, last)
    in_stages[1]()
    out_stages[3]()
    loop(steps // 4, steps, last)
    sum_start(2)
    in_stages[2]()
    sum_middle(2)
    in_stages[3]()
    out_stages[4]()
    in_stages[4]()
    ln_ref[...] = sum_finish(2)
    in_stages[5]()
    out_stages[5]()

    def finish_copies(m):
        up_copy(m, 0, None, False).wait_send()
        sized(peer_of(m), lambda rows: up_copy(m, 1, rows, False).wait_send())
        for part in range(2):
            each_out(peer_of(m), m, part, True, lambda copy: copy.wait_recv())
            each_out(me, m, part, False, lambda copy: copy.wait_send())
    loop(1, owners, finish_copies)


def finish_kernel(
    taps, per, per_out, piece, bounds,
    meta, grads_ref, arrived_ref, reduced_ref, reduced_out_ref, back_ref, ln_ref,
    out_hbm, grad_frames_ref, win_hbm, wout_hbm, taps_hbm, ln_hbm, gain_hbm, bias_hbm,
    out_ref, win_ref, wout_ref, taps_ref, ln_out_ref, gain_ref, bias_ref,
    stage, flat, sems, ends,
):
    me = lax.axis_index("bucket")
    owners, chunk, width = arrived_ref.shape
    own_rows = out_ref.shape[0]
    blocks = width // LANES
    share = win_ref.shape[0]
    wide = win_ref.shape[1] // LANES
    slots = sems.shape[0]
    span = grads_ref.shape[0] // slots
    copies = []

    def send(source, target):
        copies.append(pltpu.make_async_copy(source, target, ends.at[len(copies)]))
        copies[-1].start()

    def row_copy(i):
        source = pl.ds(pl.multiple_of(i * span, PACK), span)
        target = pl.ds(pl.multiple_of(meta[1, i] * span, PACK), span)
        return pltpu.make_async_copy(
            grads_ref.at[source], grad_frames_ref.at[target], sems.at[i]
        )

    def start(i, carry):
        row_copy(i).start()
        return carry

    lax.fori_loop(0, slots, start, 0)
    for b in range(owners):
        begin = meta[2, b]
        for c in range(blocks):
            stage[c, pl.ds(begin, bounds[b])] = arrived_ref[b, : bounds[b], lane(c)].astype(F32)
    for c in range(blocks):
        out_ref[:, lane(c)] = stage[c, :own_rows].astype(BF16)
    send(out_ref, out_hbm)

    def section(source, count, s):
        q, r = s // count, s % count
        return source[q, r * share : (r + 1) * share].astype(F32)

    for c in range(wide):
        win_ref[:, lane(c)] = section(reduced_ref, per, c)
    send(win_ref, win_hbm)
    for c in range(blocks):
        wout_ref[:, lane(c)] = section(reduced_out_ref, per_out, c)
    send(wout_ref, wout_hbm)
    row = jnp.zeros((1, share), F32)
    for j in range(owners):
        c, n = j * share // LANES, j * share % LANES
        row = jnp.where(me == j, ln_ref[c : c + 1, n : n + share], row)
    ln_out_ref[...] = row
    send(ln_out_ref, ln_hbm)
    bias_ref[...] = row_of(back_ref, 0, blocks)
    send(bias_ref, bias_hbm)
    gain_ref[...] = row_of(back_ref, blocks, blocks)
    send(gain_ref, gain_hbm)
    flat[...] = jnp.zeros_like(flat)
    for q in range(reduced_ref.shape[0]):
        flat[q * piece : (q + 1) * piece] = reduced_ref[
            q, per * share : per * share + piece
        ].astype(F32)
    taps_ref[...] = flat[...].T[:taps, :share]
    send(taps_ref, taps_hbm)

    def wait(i, carry):
        row_copy(i).wait()
        return carry

    lax.fori_loop(0, slots, wait, 0)
    for copy in copies:
        copy.wait()


def in_hbm(array):
    return pltpu.with_memory_space_constraint(array, pltpu.HBM)


def local(frames, lengths, owner_ids, upstream, ln_gain, w_in, w_dw, bn_gain, bn_bias, w_out):
    groups, owners = lax.axis_size("dp"), lax.axis_size("bucket")
    all_rows, width = frames.shape
    taps = w_dw.shape[1]
    slots = lengths.shape[1] // owners
    span = all_rows // slots
    pairs = slots // owners
    own_rows = upstream.shape[0]
    blocks = width // LANES
    wide = w_in.shape[1] // LANES
    total_frames = float(own_rows * owners * groups)
    in_vmem = pl.BlockSpec(memory_space=pltpu.VMEM)
    in_smem = pl.BlockSpec(memory_space=pltpu.SMEM)
    anywhere = pl.BlockSpec(memory_space=pl.ANY)
    group = pairs * max(1, 4 // pairs)
    size, fwd, inv, spec, corr = transform_tables(span, taps, group)
    chunk = pairs * span
    bounds = chunk_bounds(own_rows, pairs, span, owners)
    early = max(PACK, min(chunk // 2 // PACK * PACK, bounds[0] - PACK))
    early_out = max(PACK, min(chunk * 5 // 12 // PACK * PACK, bounds[0] - PACK))
    share = width // owners
    per, per_out = -(-wide // groups), -(-blocks // groups)
    piece = share // groups
    sides = groups // 2
    rows_in = (per * share + -(-piece // PACK) * PACK, LANES)
    rows_out = (per_out * share, LANES)

    meta = pl.pallas_call(
        functools.partial(tables_kernel, slots),
        in_specs=[in_smem, in_smem],
        out_specs=in_smem,
        out_shape=jax.ShapeDtypeStruct((3, slots), jnp.int32),
        scratch_shapes=[pltpu.SMEM((owners,), jnp.int32)],
        compiler_params=pltpu.CompilerParams(vmem_limit_bytes=1 << 20),
        name="tables",
    )(in_hbm(lengths), in_hbm(owner_ids))

    operands = (
        upstream, w_dw.T, spec, frames.reshape(slots, span, width), w_in, ln_gain[None], fwd, inv,
        w_out, bn_gain[None], bn_bias[None], corr,
    )
    sums_shape = (2 * blocks, LANES)
    tall = pltpu.VMEM((all_rows, width), F32)
    short = pltpu.VMEM((all_rows, width), BF16)
    chunks = pltpu.VMEM((owners, chunk, width), BF16)

    def reduce_scratch(kind):
        return [
            pltpu.VMEM((owners, sides) + kind, BF16),
            pltpu.VMEM((sides, owners) + kind, BF16),
            pltpu.VMEM((sides, owners) + kind, BF16),
            pltpu.VMEM((owners // 2, 2) + kind, BF16),
            pltpu.VMEM((owners // 2,) + kind, BF16),
            pltpu.VMEM((owners // 2,) + kind, BF16),
            pltpu.VMEM((owners // 2,) + kind, BF16),
            pltpu.VMEM(kind, BF16),
            pltpu.SemaphoreType.DMA((2, 2)),
            pltpu.SemaphoreType.DMA((2, 2 * sides)),
            pltpu.SemaphoreType.DMA((2, 1)),
            pltpu.SemaphoreType.DMA((2, owners // 2)),
            pltpu.SemaphoreType.DMA((2, groups)),
        ]

    grads, arrived, reduced, reduced_out, back, ln_total = pl.pallas_call(
        functools.partial(
            step_kernel,
            groups, owners, group, taps, size, early, early_out, bounds,
            total_frames,
        ),
        in_specs=[in_smem] + [anywhere] * 12,
        out_specs=[in_vmem] * 6,
        out_shape=[
            jax.ShapeDtypeStruct((all_rows, width), BF16),
            jax.ShapeDtypeStruct((owners, chunk, width), BF16),
            jax.ShapeDtypeStruct((groups,) + rows_in, BF16),
            jax.ShapeDtypeStruct((groups,) + rows_out, BF16),
            jax.ShapeDtypeStruct(sums_shape, F32),
            jax.ShapeDtypeStruct(sums_shape, F32),
        ],
        scratch_shapes=[pltpu.VMEM(operand.shape, operand.dtype) for operand in operands]
        + [
            pltpu.VMEM((blocks, own_rows + chunk, LANES), F32),
            chunks,
            chunks,
            chunks,
            tall,
            pltpu.VMEM((all_rows, LANES), F32),
            tall,
            tall,
            short,
            pltpu.VMEM((slots * size, width), F32),
            tall,
            tall,
            short,
            short,
            pltpu.VMEM((all_rows, w_in.shape[1]), BF16),
            pltpu.VMEM((taps + 1, width), F32),
            pltpu.VMEM((3 * size // 2, width), F32),
            pltpu.VMEM((2, SUB, width), F32),
            pltpu.VMEM((3 * size // 2, width), F32),
            pltpu.VMEM(sums_shape, F32),
            pltpu.VMEM((3,) + sums_shape, F32),
            pltpu.VMEM((3,) + sums_shape, F32),
            pltpu.VMEM((3, groups) + sums_shape, F32),
            pltpu.VMEM((3, owners) + sums_shape, F32),
            pltpu.VMEM((LANES, LANES), F32),
            pltpu.VMEM((owners, 2, sides) + rows_in, BF16),
            pltpu.VMEM((owners, 2, sides) + rows_out, BF16),
            pltpu.SemaphoreType.DMA((12,)),
            pltpu.SemaphoreType.DMA((2, owners)),
            pltpu.SemaphoreType.DMA((2, owners)),
            pltpu.SemaphoreType.DMA((2, owners)),
            pltpu.SemaphoreType.DMA((2, owners)),
            pltpu.SemaphoreType.DMA((groups,)),
            pltpu.SemaphoreType.DMA((3, groups)),
            pltpu.SemaphoreType.DMA((owners,)),
            pltpu.SemaphoreType.DMA((3, owners)),
        ]
        + reduce_scratch(rows_in)
        + reduce_scratch(rows_out),
        compiler_params=pltpu.CompilerParams(
            collective_id=0, has_side_effects=True, vmem_limit_bytes=STEP_VMEM
        ),
        cost_estimate=pl.CostEstimate(
            flops=10**10, bytes_accessed=4 * 10**7, transcendentals=0
        ),
        name="step",
    )(meta, *map(in_hbm, operands))

    results = [jax.ShapeDtypeStruct((own_rows, width), BF16)] + [
        jax.ShapeDtypeStruct(shape, F32)
        for shape in (
            (share, w_in.shape[1]), (share, width), (taps, share), (1, share), (1, width), (1, width)
        )
    ]
    out_frames, grad_frames, grad_win, grad_wo, grad_taps, grad_ln, grad_gain, grad_bias = (
        pl.pallas_call(
            functools.partial(finish_kernel, taps, per, per_out, piece, bounds),
            in_specs=[in_smem] + [in_vmem] * 6,
            out_specs=[anywhere] * 8,
            out_shape=[
                results[0],
                jax.ShapeDtypeStruct((all_rows, width), BF16),
                *results[1:],
            ],
            scratch_shapes=[pltpu.VMEM(result.shape, result.dtype) for result in results]
            + [
                pltpu.VMEM((blocks, own_rows + chunk, LANES), F32),
                pltpu.VMEM((LANES, LANES), F32),
                pltpu.SemaphoreType.DMA((slots,)),
                pltpu.SemaphoreType.DMA((len(results),)),
            ],
            compiler_params=pltpu.CompilerParams(vmem_limit_bytes=8 << 20),
            name="finish",
        )(meta, grads, arrived, reduced, reduced_out, back, ln_total)
    )
    return (
        out_frames,
        grad_frames,
        grad_win,
        grad_wo,
        grad_taps.T,
        grad_ln[0],
        grad_gain[0],
        grad_bias[0],
    )


def solution(mesh):
    placed = (
        P(("dp", "bucket"), None),
        P("dp", None),
        P("dp", None),
        P(("dp", "bucket"), None),
        P(),
        P(),
        P(),
        P(),
        P(),
        P(),
    )
    return jax.shard_map(
        local,
        mesh=mesh,
        in_specs=placed,
        out_specs=(
            P(("dp", "bucket"), None),
            P(("dp", "bucket"), None),
            P("bucket", None),
            P("bucket", None),
            P("bucket", None),
            P("bucket"),
            P(),
            P(),
        ),
        check_vma=False,
    )
```

```python
import functools

import jax
import jax.numpy as jnp
import numpy as np
from jax import lax
from jax.experimental import pallas as pl
from jax.experimental.pallas import tpu as pltpu
from jax.sharding import PartitionSpec as P

EPSILON = 1e-05
LANES = 128
SUB = 8
PACK = 16
STEP_VMEM = 50 << 20
MESH = pl.DeviceIdType.MESH
BF16 = jnp.bfloat16
F32 = jnp.float32


def lane(c):
    return slice(c * LANES, (c + 1) * LANES)


def row_of(packed, first, blocks):
    return jnp.concatenate([packed[first + c : first + c + 1] for c in range(blocks)], axis=1)


def keep_live(values, lengths, span):
    position = lax.broadcasted_iota(jnp.int32, (span, values.shape[1]), 0)
    parts = [
        jnp.where(position < length, values[i * span : (i + 1) * span], 0.0)
        for i, length in enumerate(lengths)
    ]
    return jnp.concatenate(parts, axis=0)


def fold_rows(values):
    rows, width = values.shape
    return jnp.sum(values.reshape(rows // SUB, SUB, width), axis=0)


def matmul(a, b):
    return jnp.dot(a, b, preferred_element_type=F32)


def matmul_nt(a, b):
    return lax.dot_general(a, b, (((1,), (1,)), ((), ())), preferred_element_type=F32)


def matmul_tn(a, b):
    return lax.dot_general(a, b, (((0,), (0,)), ((), ())), preferred_element_type=F32)


def matmul_exact(a, b):
    return jnp.dot(a, b, preferred_element_type=F32, precision=lax.Precision.HIGHEST)


def transform_tables(span, taps, group):
    size = -(-(span + taps // 2) // (2 * PACK)) * (2 * PACK)
    half = size // 2
    freq = np.arange(half)[:, None]

    def angle(times):
        return 2.0 * np.pi * freq * np.asarray(times)[None, :] / size

    def flip(times):
        return np.where(np.asarray(times) % 2 == 0, 1.0, -1.0)

    times = np.arange(span)
    real, imag = np.cos(angle(times)), -np.sin(angle(times))
    imag[0] = flip(times)
    forward = np.concatenate([real, imag], axis=0)
    scale = np.where(np.arange(size) % half == 0, 1.0, 2.0) / size
    inverse = (forward * scale[:, None]).T
    lags = taps // 2 - np.arange(taps)
    wr, wi, wn = np.cos(angle(lags)), -np.sin(angle(lags)), np.cos(angle(lags))
    wi[0] = 0.0
    wn[0] = flip(lags)
    spectrum = np.concatenate([wr, wi, wn], axis=0)
    spectrum = np.pad(spectrum, ((0, 0), (0, 1)))
    back = -lags
    cr, cn, ci = np.cos(angle(back)), np.cos(angle(back)), -np.sin(angle(back))
    cn[0] = flip(back)
    ci[0] = 0.0
    both = np.concatenate([scale[:half], scale[half:], scale[half:]])
    correlate = (np.concatenate([cr, cn, ci], axis=0) * both[:, None]).T
    correlate = np.pad(correlate, ((0, 1), (0, 0)))
    eye = np.eye(group)
    return (
        size,
        jnp.asarray(np.kron(eye, forward), BF16),
        jnp.asarray(np.kron(eye, inverse), BF16),
        jnp.asarray(spectrum, F32),
        jnp.asarray(correlate, F32),
    )


def chunk_bounds(own_rows, pairs, span, loaders):
    rows = [min(pairs * span, (own_rows - b * pairs) // (loaders - b)) for b in range(loaders)]
    return [-(-r // PACK) * PACK for r in rows]


def tables_kernel(slots, lens_ref, owners_ref, meta_ref, counts):
    me = lax.axis_index("bucket")
    loaders = lens_ref.shape[1] // slots
    pairs = slots // loaders

    def look(b, start):
        meta_ref[2, b] = start
        for j in range(slots):
            at = b * slots + j
            start = start + jnp.where(owners_ref[0, at] == me, lens_ref[0, at], 0)
        return start

    lax.fori_loop(0, loaders, look, jnp.int32(0))

    def clear(i, carry):
        counts[i] = 0
        return carry

    lax.fori_loop(0, loaders, clear, 0)

    def place(i, carry):
        owner = owners_ref[0, me * slots + i]
        rank = counts[owner]
        counts[owner] = rank + 1
        at = owner * pairs + rank
        meta_ref[0, at] = lens_ref[0, me * slots + i]
        meta_ref[1, at] = i
        return carry

    lax.fori_loop(0, slots, place, 0)


def reducer(groups, owners, dp, me, src, out, refs):
    first, first_sum, second, second_sum, twin, twin_sum, third, mine = refs[:8]
    core_sems, pair_sems, twin_sems, row_sems, all_sems = refs[8:]
    sides = groups // 2
    core, side = lax.rem(dp, 2), dp // 2
    partner = side * 2 + (1 - core)

    def remote(source, target, sems, i, j, device):
        return pltpu.make_async_remote_copy(
            src_ref=source,
            dst_ref=target,
            send_sem=sems.at[0, i],
            recv_sem=sems.at[1, j],
            device_id=device,
            device_id_type=MESH,
        )

    wave = owners // 2

    def wave_of(h):
        return pl.ds(h * wave, wave)

    def swap(h):
        return remote(
            src.at[wave_of(h), 1 - core], first.at[wave_of(h)], core_sems, h, h, (partner, me)
        )

    def to_side(h, n, arriving):
        other = lax.rem(side + (sides - n if arriving else n), sides)
        slot = other if arriving else side
        target = lax.rem(side + n, sides)
        return remote(
            first_sum.at[target, wave_of(h)], second.at[slot, wave_of(h)], pair_sems,
            h * sides + n, h * sides + n, (target * 2 + core, me),
        )

    near = lax.rem(me, 2)
    mate = me + 1 - 2 * near
    pairs = owners // 2

    def pair_of(i):
        return lax.rem(me // 2 + 1 + i, pairs)

    def to_mate():
        return remote(second_sum.at[:, 1 - near], twin, twin_sems, 0, 0, (dp, mate))

    def to_owner(i, arriving):
        pair = lax.rem(me // 2 + i, pairs)
        slot = pair if arriving else me // 2
        return remote(
            twin_sum.at[pair], third.at[slot], row_sems, i, slot, (dp, pair * 2 + near)
        )

    def to_group(i, arriving):
        other = lax.rem(dp + i, groups)
        device = other if arriving else dp
        slot = lax.rem(device, 2) * sides + device // 2
        return remote(mine, out.at[slot], all_sems, i, slot, (other, me))

    def loop(low, high, body):
        def step(i, carry):
            body(i)
            return carry

        lax.fori_loop(low, high, step, 0)

    def stage_swap(h):
        swap(h).start()

    def add_first(i):
        total = src[i, core].astype(F32) + first[i].astype(F32)
        for n in range(sides):
            first_sum[n, i] = total[n].astype(BF16)

    def stage_side():
        for h in range(2):
            swap(h).wait_recv()
            loop(h * wave, (h + 1) * wave, add_first)
            for n in range(1, sides):
                to_side(h, n, False).start()

    def add_second(i):
        for half in range(2):
            bucket = i * 2 + half
            total = first_sum[side, bucket].astype(F32)
            for n in range(1, sides):
                total = total + second[lax.rem(side + n, sides), bucket].astype(F32)
            second_sum[i, half] = total.astype(BF16)

    def stage_mate():
        for h in range(2):
            for n in range(1, sides):
                to_side(h, n, True).wait_recv()
        loop(0, pairs, add_second)
        to_mate().start()

    def add_twin(i):
        pair = pair_of(i)
        total = second_sum[pair, near].astype(F32) + twin[pair].astype(F32)
        twin_sum[pair] = total.astype(BF16)

    def twin_and_send(i):
        add_twin(i)
        to_owner(i + 1, False).start()

    def stage_owner():
        to_mate().wait_recv()
        loop(0, pairs - 1, twin_and_send)
        add_twin(pairs - 1)
        third[me // 2] = twin_sum[me // 2]

    def stage_group():
        loop(1, pairs, lambda i: to_owner(i, True).wait_recv())
        total = lax.fori_loop(
            1, pairs, lambda i, t: t + third[i].astype(F32), third[0].astype(F32)
        )
        mine[...] = total.astype(BF16)
        loop(1, groups, lambda i: to_group(i, False).start())
        out[core * sides + side] = mine[...]

    def stage_end():
        loop(1, groups, lambda i: to_group(i, True).wait_recv())

        for h in range(2):
            swap(h).wait_send()
            for n in range(1, sides):
                to_side(h, n, False).wait_send()
        to_mate().wait_send()
        loop(1, pairs, lambda i: to_owner(i, False).wait_send())
        loop(1, groups, lambda i: to_group(i, False).wait_send())

    return stage_swap, stage_side, stage_mate, stage_owner, stage_group, stage_end


def step_kernel(
    groups, owners, group, taps, size, early, early_out, bounds, total_frames,
    meta, *refs,
):
    sources, refs = refs[:12], refs[12:]
    grads_ref, arrived_ref, reduced_ref, reduced_out_ref, back_ref, ln_ref = refs[:6]
    targets, refs = refs[6:18], refs[18:]
    up, w_dw_ref, spec_ref, frames, w_in_ref, gain_ref, fwd_ref, inv_ref = targets[:8]
    w_out_ref, bn_gain_ref, bn_bias_ref, corr_ref = targets[8:]
    (
    stage, outgoing, arrive, outbuf,
    normed_s, inverse_s, linear_s, gate_s, h_s, spect_s, conv_s, fac_s, sw_s, dy_s, ga_s,
    w_taps, wspec, acc, xacc, tot, parts, mids, slots_a, slots_b, flat,
    packed, packed_out, local_sems, up_send, up_recv, out_send, out_recv,
    a_send, a_recv, b_send, b_recv, *reduce_refs,
    ) = refs
    dp, me = lax.axis_index("dp"), lax.axis_index("bucket")
    slot_count, span, width = frames.shape
    all_rows = slot_count * span
    own_rows = up.shape[0]
    blocks = width // LANES
    wide = w_in_ref.shape[1] // LANES
    chunk = all_rows // owners
    pairs = slot_count // owners
    steps = slot_count // group
    held = group // pairs
    grows = group * span
    half = size // 2
    far = owners // 2
    barrier = pltpu.get_barrier_semaphore()

    def loop(low, high, body):
        def step(i, carry):
            body(i)
            return carry

        lax.fori_loop(low, high, step, 0)

    def peer_of(m):
        bits = range((owners - 1).bit_length())
        return sum(lax.rem(me // 2**k + m // 2**k, 2) * 2**k for k in bits)

    def greet_group(i):
        pl.semaphore_signal(
            barrier, inc=1, device_id=(lax.rem(dp + i, groups), me), device_id_type=MESH
        )

    def greet_owner(m):
        pl.semaphore_signal(barrier, inc=1, device_id=(dp, peer_of(m)), device_id_type=MESH)

    loop(1, groups, greet_group)
    loop(1, owners, greet_owner)
    loads = [
        pltpu.make_async_copy(source, target, local_sems.at[n])
        for n, (source, target) in enumerate(zip(sources, targets))
    ]
    for load in loads:
        load.start()

    loads[0].wait()
    for c in range(blocks):
        stage[c, :own_rows] = up[:, lane(c)].astype(F32)
        stage[c, own_rows:] = jnp.zeros((chunk, LANES), F32)

    def lay_out(b, low, high):
        start = meta[2, b] + low
        for c in range(blocks):
            outgoing[b, low:high, lane(c)] = stage[c, pl.ds(start, high - low)].astype(BF16)

    loop(0, owners, lambda b: lay_out(b, 0, early))

    def sized(index, body):
        for rows in sorted(set(bounds)):
            low = bounds.index(rows)
            high = low + bounds.count(rows)

            @pl.when(jnp.logical_and(index >= low, index < high))
            def _():
                body(rows)

    def up_copy(m, part, rows, arriving):
        peer = peer_of(m)
        slot = peer if arriving else me
        span_of = pl.ds(0, early) if part == 0 else pl.ds(early, rows - early)
        return pltpu.make_async_remote_copy(
            src_ref=outgoing.at[peer, span_of],
            dst_ref=arrive.at[slot, span_of],
            send_sem=up_send.at[part, m],
            recv_sem=up_recv.at[part, m],
            device_id=(dp, peer),
            device_id_type=MESH,
        )

    cuts = (0, early_out, chunk)

    def out_copy(m, part, rows, arriving):
        peer = peer_of(m)
        slot = peer if arriving else me
        low, high = cuts[part], min(cuts[part + 1], rows)
        return pltpu.make_async_remote_copy(
            src_ref=outbuf.at[peer, pl.ds(low, high - low)],
            dst_ref=arrived_ref.at[slot, pl.ds(low, high - low)],
            send_sem=out_send.at[part, m],
            recv_sem=out_recv.at[part, m],
            device_id=(dp, peer),
            device_id_type=MESH,
        )

    def each_out(loader, m, part, arriving, use):
        def body(rows):
            if rows > cuts[part]:
                use(out_copy(m, part, rows, arriving))

        sized(loader, body)

    def start_out(low, high, part):
        loop(
            low,
            high,
            lambda j: each_out(me, owners - 1 - j, part, False, lambda copy: copy.start()),
        )

    def start_up(part):
        def body(j):
            m = owners - 1 - j
            if part == 0:
                up_copy(m, 0, None, False).start()
            else:
                sized(peer_of(m), lambda rows: up_copy(m, 1, rows, False).start())

        loop(0, owners - 1, body)

    def a_copy(n, i, arriving):
        other = lax.rem(dp + i, groups)
        slot = lax.rem(dp + groups - i, groups) if arriving else dp
        return pltpu.make_async_remote_copy(
            src_ref=parts.at[n],
            dst_ref=slots_a.at[n, slot],
            send_sem=a_send.at[i],
            recv_sem=a_recv.at[n, i],
            device_id=(other, me),
            device_id_type=MESH,
        )

    def b_copy(n, m, arriving):
        peer = peer_of(m)
        slot = peer if arriving else me
        return pltpu.make_async_remote_copy(
            src_ref=mids.at[n],
            dst_ref=slots_b.at[n, slot],
            send_sem=b_send.at[m],
            recv_sem=b_recv.at[n, m],
            device_id=(dp, peer),
            device_id_type=MESH,
        )

    def sum_start(n):
        for k in range(2):
            row = jnp.sum(acc[k], axis=0, keepdims=True)
            for c in range(blocks):
                parts[n, k * blocks + c : k * blocks + c + 1] = row[:, lane(c)]
        loop(1, groups, lambda i: a_copy(n, i, False).start())
        slots_a[n, dp] = parts[n]

    def sum_middle(n):
        loop(1, groups, lambda i: a_copy(n, i, True).wait_recv())
        mids[n] = lax.fori_loop(1, groups, lambda i, t: t + slots_a[n, i], slots_a[n, 0])
        loop(0, owners - 1, lambda j: b_copy(n, owners - 1 - j, False).start())
        slots_b[n, me] = mids[n]

    def sum_finish(n):
        loop(1, owners, lambda m: b_copy(n, m, True).wait_recv())
        loop(1, groups, lambda i: a_copy(n, i, False).wait_send())
        loop(1, owners, lambda m: b_copy(n, m, False).wait_send())
        return lax.fori_loop(1, owners, lambda i, t: t + slots_b[n, i], slots_b[n, 0])

    loads[1].wait()
    loads[2].wait()
    w_taps[...] = jnp.zeros_like(w_taps)
    w_taps[:taps] = w_dw_ref[...]
    wspec[...] = matmul_exact(spec_ref[...], w_taps[...])
    acc[...] = jnp.zeros_like(acc)
    pl.semaphore_wait(barrier, groups + owners - 2)
    start_up(0)
    loop(0, owners, lambda b: lay_out(b, early, chunk))
    arrive[me] = outgoing[me]
    for load in loads[3:8]:
        load.wait()

    def rows_of(i):
        return pl.ds(pl.multiple_of(i * grows, PACK), grows)

    def spec_rows(i):
        return pl.ds(pl.multiple_of(i * group * size, PACK), group * size)

    def lengths_of(i):
        return [meta[0, i * group + u] for u in range(group)]

    def packing(lengths):
        column = lax.broadcasted_iota(jnp.int32, (1, grows), 1)
        target = jnp.full((1, grows), -1, jnp.int32)
        for u in range(group):
            first = (u // pairs) * chunk + sum(lengths[u - u % pairs : u], jnp.int32(0))
            at = column - u * span
            live = jnp.logical_and(at >= 0, at < lengths[u])
            target = jnp.where(live, at + first, target)
        row = lax.broadcasted_iota(jnp.int32, (grows, grows), 0)
        return jnp.where(row == target, 1.0, 0.0).astype(BF16)

    def forward(i):
        rows = rows_of(i)
        lengths = lengths_of(i)
        values = jnp.concatenate(
            [frames[meta[1, i * group + u]] for u in range(group)], axis=0
        ).astype(F32)
        centred = values - jnp.mean(values, axis=1, keepdims=True)
        inverse = lax.rsqrt(jnp.mean(centred * centred, axis=1, keepdims=True) + EPSILON)
        normed = centred * inverse
        h = (normed * gain_ref[...]).astype(BF16)
        projected = matmul(h, w_in_ref[...])
        linear, gate = projected[:, :width], jax.nn.sigmoid(projected[:, width:])
        normed_s[rows] = normed
        inverse_s[rows] = jnp.broadcast_to(inverse, (grows, LANES))
        linear_s[rows] = linear
        gate_s[rows] = gate
        h_s[rows] = h
        gated = keep_live(linear * gate, lengths, span).astype(BF16)
        spect = matmul(fwd_ref[...], gated)
        spect_s[spec_rows(i)] = spect
        wr, wi, wn = wspec[:half], wspec[half : 2 * half], wspec[2 * half :]
        mixed = []
        for u in range(group):
            re = spect[u * size : u * size + half]
            im = spect[u * size + half : (u + 1) * size]
            mixed.append((wr * re - wi * im).astype(BF16))
            mixed.append((wn * im + wi * re).astype(BF16))
        conv = matmul(inv_ref[...], jnp.concatenate(mixed, axis=0))
        conv_s[rows] = conv
        masked = keep_live(conv, lengths, span)
        acc[0] += fold_rows(masked)
        acc[1] += fold_rows(masked * masked)

    loop(0, steps, forward)
    sum_start(0)
    sum_middle(0)
    for load in loads[8:]:
        load.wait()
    tot[...] = sum_finish(0)
    start_up(1)
    centre = row_of(tot, 0, blocks) / total_frames
    variance = row_of(tot, blocks, blocks) / total_frames - centre * centre
    bn_inverse = lax.rsqrt(variance + EPSILON)
    acc[...] = jnp.zeros_like(acc)
    bn_gain, bn_bias = bn_gain_ref[...], bn_bias_ref[...]

    def swish(i):
        rows = rows_of(i)
        bn_normed = (conv_s[rows] - centre) * bn_inverse
        conv_s[rows] = bn_normed
        bn = bn_normed * bn_gain + bn_bias
        sig = jax.nn.sigmoid(bn)
        swished = (bn * sig).astype(BF16)
        sw_s[rows] = swished
        fac_s[rows] = sig * (1.0 + bn * (1.0 - sig))
        out = matmul(swished, w_out_ref[...]).astype(BF16)
        out = matmul(packing(lengths_of(i)), out).astype(BF16)
        for r in range(held):
            outbuf[i * held + r] = out[r * chunk : (r + 1) * chunk]

    loop(0, steps, swish)

    @pl.when(me >= far)
    def _():
        start_out(0, far, 0)

    def middle(t):
        m = lax.rem(owners - t * held, owners)
        i = peer_of(m) // held
        rows = rows_of(i)
        lengths = lengths_of(i)
        for r in range(held):
            owner = i * held + r
            bits = range((owners - 1).bit_length())
            gap = sum(lax.rem(me // 2**k + owner // 2**k, 2) * 2**k for k in bits)

            @pl.when(owner != me)
            def _():
                up_copy(gap, 0, None, True).wait_recv()
                sized(me, lambda rows: up_copy(gap, 1, rows, True).wait_recv())

        pieces = []
        position = lax.broadcasted_iota(jnp.int32, (chunk, width), 0)
        for r in range(held):
            total = sum(lengths[r * pairs : (r + 1) * pairs], jnp.int32(0))
            came = arrive[i * held + r].astype(F32)
            pieces.append(jnp.where(position < total, came, 0.0).astype(BF16))
        dy = matmul_tn(packing(lengths), jnp.concatenate(pieces, axis=0)).astype(BF16)
        dy_s[rows] = dy
        grad_bn = matmul_nt(dy, w_out_ref[...]) * fac_s[rows]
        fac_s[rows] = grad_bn
        acc[0] += fold_rows(grad_bn)
        acc[1] += fold_rows(grad_bn * conv_s[rows])

    loop(0, steps, middle)
    sum_start(1)
    sum_middle(1)

    arrived_ref[me] = outbuf[me]

    share = width // owners
    per, per_out = -(-wide // groups), -(-blocks // groups)
    piece = share // groups
    sides = groups // 2
    in_stages = reducer(groups, owners, dp, me, packed, reduced_ref, reduce_refs[:13])
    out_stages = reducer(groups, owners, dp, me, packed_out, reduced_out_ref, reduce_refs[13:])

    def put(target, count, j, section, block):
        q, r = section // count, section % count
        target[j, q // sides, q % sides, r * share : (r + 1) * share] = block.astype(BF16)

    if per_out * groups != blocks:
        packed_out[...] = jnp.zeros_like(packed_out)
    if per * groups != wide or packed.shape[3] != per * share + piece:
        packed[...] = jnp.zeros_like(packed)
    for c in range(blocks):
        grad = matmul_tn(sw_s[:, lane(c)], dy_s[...])
        for n in range(LANES // share):
            j = c * (LANES // share) + n
            for s in range(blocks):
                put(packed_out, per_out, j, s, grad[n * share : (n + 1) * share, lane(s)])
        if c % (blocks // 2) == blocks // 2 - 1:
            out_stages[0](c // (blocks // 2))
    back_ref[...] = sum_finish(1)

    @pl.when(me < far)
    def _():
        start_out(0, far, 0)

    start_out(0, far, 1)
    start_out(far, owners - 1, 0)
    start_out(far, owners - 1, 1)
    bias_mean = row_of(back_ref, 0, blocks) / total_frames
    gain_mean = row_of(back_ref, blocks, blocks) / total_frames
    scale = bn_gain * bn_inverse
    xacc[...] = jnp.zeros_like(xacc)

    def backward(i):
        rows = rows_of(i)
        lengths = lengths_of(i)
        grad_conv = scale * (fac_s[rows] - bias_mean - conv_s[rows] * gain_mean)
        grad_conv = keep_live(grad_conv, lengths, span).astype(BF16)
        spect = matmul(fwd_ref[...], grad_conv)
        saved = spect_s[spec_rows(i)]
        wr, wi, wn = wspec[:half], wspec[half : 2 * half], wspec[2 * half :]
        mixed, terms = [], [None] * 3
        for u in range(group):
            re = spect[u * size : u * size + half]
            im = spect[u * size + half : (u + 1) * size]
            sre = saved[u * size : u * size + half]
            sim = saved[u * size + half : (u + 1) * size]
            mixed.append((wr * re + wi * im).astype(BF16))
            mixed.append((wn * im - wi * re).astype(BF16))
            new = (re * sre, im * sim, re * sim - im * sre)
            terms = [b if a is None else a + b for a, b in zip(terms, new)]
        for n in range(3):
            xacc[n * half : (n + 1) * half] += terms[n]
        grad_gated = matmul(inv_ref[...], jnp.concatenate(mixed, axis=0))
        grad_gated = keep_live(grad_gated, lengths, span)
        gate = gate_s[rows]
        left = grad_gated * gate
        ga_s[rows, :width] = left.astype(BF16)
        ga_s[rows, width:] = (left * linear_s[rows] * (1.0 - gate)).astype(BF16)

    def twice(body):
        def both(i):
            body(2 * i)
            body(2 * i + 1)

        return both

    loop(0, steps // 4, twice(backward))
    out_stages[1]()
    loop(steps // 4, steps // 2, twice(backward))
    out_stages[2]()
    grad_taps = matmul_exact(corr_ref[...], xacc[...])
    flat[...] = jnp.zeros_like(flat)
    for c in range(blocks):
        grad = matmul_tn(h_s[:, lane(c)], ga_s[...])
        flat[: taps + 1] = grad_taps[:, lane(c)]
        turned = flat[...].T.astype(BF16)
        for n in range(LANES // share):
            j = c * (LANES // share) + n
            for s in range(wide):
                put(packed, per, j, s, grad[n * share : (n + 1) * share, lane(s)])
            for q in range(groups):
                packed[j, q // sides, q % sides, per * share : per * share + piece] = turned[
                    n * share + q * piece : n * share + (q + 1) * piece
                ]
        if c % (blocks // 2) == blocks // 2 - 1:
            in_stages[0](c // (blocks // 2))
    acc[...] = jnp.zeros_like(acc)

    def last(i):
        rows = rows_of(i)
        lengths = lengths_of(i)
        grad_h = matmul_nt(ga_s[rows], w_in_ref[...])
        normed, inverse = normed_s[rows], inverse_s[rows][:, :1]
        acc[0] += fold_rows(grad_h * normed)
        scaled = grad_h * gain_ref[...]
        inner_mean = jnp.mean(scaled * normed, axis=1, keepdims=True)
        grad_x = inverse * (scaled - jnp.mean(scaled, axis=1, keepdims=True) - normed * inner_mean)
        grads_ref[rows] = keep_live(grad_x, lengths, span).astype(BF16)

    loop(0, steps // 4, last)
    in_stages[1]()
    out_stages[3]()
    loop(steps // 4, steps, last)
    sum_start(2)
    in_stages[2]()
    sum_middle(2)
    in_stages[3]()
    out_stages[4]()
    in_stages[4]()
    ln_ref[...] = sum_finish(2)
    in_stages[5]()
    out_stages[5]()

    def finish_copies(m):
        up_copy(m, 0, None, False).wait_send()
        sized(peer_of(m), lambda rows: up_copy(m, 1, rows, False).wait_send())
        for part in range(2):
            each_out(peer_of(m), m, part, True, lambda copy: copy.wait_recv())
            each_out(me, m, part, False, lambda copy: copy.wait_send())
    loop(1, owners, finish_copies)


def finish_kernel(
    taps, per, per_out, piece, bounds,
    meta, grads_ref, arrived_ref, reduced_ref, reduced_out_ref, back_ref, ln_ref,
    out_hbm, grad_frames_ref, win_hbm, wout_hbm, taps_hbm, ln_hbm, gain_hbm, bias_hbm,
    out_ref, win_ref, wout_ref, taps_ref, ln_out_ref, gain_ref, bias_ref,
    stage, flat, sems, ends,
):
    me = lax.axis_index("bucket")
    owners, chunk, width = arrived_ref.shape
    own_rows = out_ref.shape[0]
    blocks = width // LANES
    share = win_ref.shape[0]
    wide = win_ref.shape[1] // LANES
    slots = sems.shape[0]
    span = grads_ref.shape[0] // slots
    copies = []

    def send(source, target):
        copies.append(pltpu.make_async_copy(source, target, ends.at[len(copies)]))
        copies[-1].start()

    def row_copy(i):
        source = pl.ds(pl.multiple_of(i * span, PACK), span)
        target = pl.ds(pl.multiple_of(meta[1, i] * span, PACK), span)
        return pltpu.make_async_copy(
            grads_ref.at[source], grad_frames_ref.at[target], sems.at[i]
        )

    def start(i, carry):
        row_copy(i).start()
        return carry

    lax.fori_loop(0, slots, start, 0)
    for b in range(owners):
        begin = meta[2, b]
        for c in range(blocks):
            stage[c, pl.ds(begin, bounds[b])] = arrived_ref[b, : bounds[b], lane(c)].astype(F32)
    for c in range(blocks):
        out_ref[:, lane(c)] = stage[c, :own_rows].astype(BF16)
    send(out_ref, out_hbm)

    def section(source, count, s):
        q, r = s // count, s % count
        return source[q, r * share : (r + 1) * share].astype(F32)

    for c in range(wide):
        win_ref[:, lane(c)] = section(reduced_ref, per, c)
    send(win_ref, win_hbm)
    for c in range(blocks):
        wout_ref[:, lane(c)] = section(reduced_out_ref, per_out, c)
    send(wout_ref, wout_hbm)
    row = jnp.zeros((1, share), F32)
    for j in range(owners):
        c, n = j * share // LANES, j * share % LANES
        row = jnp.where(me == j, ln_ref[c : c + 1, n : n + share], row)
    ln_out_ref[...] = row
    send(ln_out_ref, ln_hbm)
    bias_ref[...] = row_of(back_ref, 0, blocks)
    send(bias_ref, bias_hbm)
    gain_ref[...] = row_of(back_ref, blocks, blocks)
    send(gain_ref, gain_hbm)
    flat[...] = jnp.zeros_like(flat)
    for q in range(reduced_ref.shape[0]):
        flat[q * piece : (q + 1) * piece] = reduced_ref[
            q, per * share : per * share + piece
        ].astype(F32)
    taps_ref[...] = flat[...].T[:taps, :share]
    send(taps_ref, taps_hbm)

    def wait(i, carry):
        row_copy(i).wait()
        return carry

    lax.fori_loop(0, slots, wait, 0)
    for copy in copies:
        copy.wait()


def in_hbm(array):
    return pltpu.with_memory_space_constraint(array, pltpu.HBM)


def local(frames, lengths, owner_ids, upstream, ln_gain, w_in, w_dw, bn_gain, bn_bias, w_out):
    groups, owners = lax.axis_size("dp"), lax.axis_size("bucket")
    all_rows, width = frames.shape
    taps = w_dw.shape[1]
    slots = lengths.shape[1] // owners
    span = all_rows // slots
    pairs = slots // owners
    own_rows = upstream.shape[0]
    blocks = width // LANES
    wide = w_in.shape[1] // LANES
    total_frames = float(own_rows * owners * groups)
    in_vmem = pl.BlockSpec(memory_space=pltpu.VMEM)
    in_smem = pl.BlockSpec(memory_space=pltpu.SMEM)
    anywhere = pl.BlockSpec(memory_space=pl.ANY)
    group = pairs * max(1, 4 // pairs)
    size, fwd, inv, spec, corr = transform_tables(span, taps, group)
    chunk = pairs * span
    bounds = chunk_bounds(own_rows, pairs, span, owners)
    early = max(PACK, min(chunk // 2 // PACK * PACK, bounds[0] - PACK))
    early_out = max(PACK, min(chunk * 5 // 12 // PACK * PACK, bounds[0] - PACK))
    share = width // owners
    per, per_out = -(-wide // groups), -(-blocks // groups)
    piece = share // groups
    sides = groups // 2
    rows_in = (per * share + -(-piece // PACK) * PACK, LANES)
    rows_out = (per_out * share, LANES)

    meta = pl.pallas_call(
        functools.partial(tables_kernel, slots),
        in_specs=[in_smem, in_smem],
        out_specs=in_smem,
        out_shape=jax.ShapeDtypeStruct((3, slots), jnp.int32),
        scratch_shapes=[pltpu.SMEM((owners,), jnp.int32)],
        compiler_params=pltpu.CompilerParams(vmem_limit_bytes=1 << 20),
        name="tables",
    )(in_hbm(lengths), in_hbm(owner_ids))

    operands = (
        upstream, w_dw.T, spec, frames.reshape(slots, span, width), w_in, ln_gain[None], fwd, inv,
        w_out, bn_gain[None], bn_bias[None], corr,
    )
    sums_shape = (2 * blocks, LANES)
    tall = pltpu.VMEM((all_rows, width), F32)
    short = pltpu.VMEM((all_rows, width), BF16)
    chunks = pltpu.VMEM((owners, chunk, width), BF16)

    def reduce_scratch(kind):
        return [
            pltpu.VMEM((owners, sides) + kind, BF16),
            pltpu.VMEM((sides, owners) + kind, BF16),
            pltpu.VMEM((sides, owners) + kind, BF16),
            pltpu.VMEM((owners // 2, 2) + kind, BF16),
            pltpu.VMEM((owners // 2,) + kind, BF16),
            pltpu.VMEM((owners // 2,) + kind, BF16),
            pltpu.VMEM((owners // 2,) + kind, BF16),
            pltpu.VMEM(kind, BF16),
            pltpu.SemaphoreType.DMA((2, 2)),
            pltpu.SemaphoreType.DMA((2, 2 * sides)),
            pltpu.SemaphoreType.DMA((2, 1)),
            pltpu.SemaphoreType.DMA((2, owners // 2)),
            pltpu.SemaphoreType.DMA((2, groups)),
        ]

    grads, arrived, reduced, reduced_out, back, ln_total = pl.pallas_call(
        functools.partial(
            step_kernel,
            groups, owners, group, taps, size, early, early_out, bounds,
            total_frames,
        ),
        in_specs=[in_smem] + [anywhere] * 12,
        out_specs=[in_vmem] * 6,
        out_shape=[
            jax.ShapeDtypeStruct((all_rows, width), BF16),
            jax.ShapeDtypeStruct((owners, chunk, width), BF16),
            jax.ShapeDtypeStruct((groups,) + rows_in, BF16),
            jax.ShapeDtypeStruct((groups,) + rows_out, BF16),
            jax.ShapeDtypeStruct(sums_shape, F32),
            jax.ShapeDtypeStruct(sums_shape, F32),
        ],
        scratch_shapes=[pltpu.VMEM(operand.shape, operand.dtype) for operand in operands]
        + [
            pltpu.VMEM((blocks, own_rows + chunk, LANES), F32),
            chunks,
            chunks,
            chunks,
            tall,
            pltpu.VMEM((all_rows, LANES), F32),
            tall,
            tall,
            short,
            pltpu.VMEM((slots * size, width), F32),
            tall,
            tall,
            short,
            short,
            pltpu.VMEM((all_rows, w_in.shape[1]), BF16),
            pltpu.VMEM((taps + 1, width), F32),
            pltpu.VMEM((3 * size // 2, width), F32),
            pltpu.VMEM((2, SUB, width), F32),
            pltpu.VMEM((3 * size // 2, width), F32),
            pltpu.VMEM(sums_shape, F32),
            pltpu.VMEM((3,) + sums_shape, F32),
            pltpu.VMEM((3,) + sums_shape, F32),
            pltpu.VMEM((3, groups) + sums_shape, F32),
            pltpu.VMEM((3, owners) + sums_shape, F32),
            pltpu.VMEM((LANES, LANES), F32),
            pltpu.VMEM((owners, 2, sides) + rows_in, BF16),
            pltpu.VMEM((owners, 2, sides) + rows_out, BF16),
            pltpu.SemaphoreType.DMA((12,)),
            pltpu.SemaphoreType.DMA((2, owners)),
            pltpu.SemaphoreType.DMA((2, owners)),
            pltpu.SemaphoreType.DMA((2, owners)),
            pltpu.SemaphoreType.DMA((2, owners)),
            pltpu.SemaphoreType.DMA((groups,)),
            pltpu.SemaphoreType.DMA((3, groups)),
            pltpu.SemaphoreType.DMA((owners,)),
            pltpu.SemaphoreType.DMA((3, owners)),
        ]
        + reduce_scratch(rows_in)
        + reduce_scratch(rows_out),
        compiler_params=pltpu.CompilerParams(
            collective_id=0, has_side_effects=True, vmem_limit_bytes=STEP_VMEM
        ),
        cost_estimate=pl.CostEstimate(
            flops=10**10, bytes_accessed=4 * 10**7, transcendentals=0
        ),
        name="step",
    )(meta, *map(in_hbm, operands))

    results = [jax.ShapeDtypeStruct((own_rows, width), BF16)] + [
        jax.ShapeDtypeStruct(shape, F32)
        for shape in (
            (share, w_in.shape[1]), (share, width), (taps, share), (1, share), (1, width), (1, width)
        )
    ]
    out_frames, grad_frames, grad_win, grad_wo, grad_taps, grad_ln, grad_gain, grad_bias = (
        pl.pallas_call(
            functools.partial(finish_kernel, taps, per, per_out, piece, bounds),
            in_specs=[in_smem] + [in_vmem] * 6,
            out_specs=[anywhere] * 8,
            out_shape=[
                results[0],
                jax.ShapeDtypeStruct((all_rows, width), BF16),
                *results[1:],
            ],
            scratch_shapes=[pltpu.VMEM(result.shape, result.dtype) for result in results]
            + [
                pltpu.VMEM((blocks, own_rows + chunk, LANES), F32),
                pltpu.VMEM((LANES, LANES), F32),
                pltpu.SemaphoreType.DMA((slots,)),
                pltpu.SemaphoreType.DMA((len(results),)),
            ],
            compiler_params=pltpu.CompilerParams(vmem_limit_bytes=8 << 20),
            name="finish",
        )(meta, grads, arrived, reduced, reduced_out, back, ln_total)
    )
    return (
        out_frames,
        grad_frames,
        grad_win,
        grad_wo,
        grad_taps.T,
        grad_ln[0],
        grad_gain[0],
        grad_bias[0],
    )


def solution(mesh):
    placed = (
        P(("dp", "bucket"), None),
        P("dp", None),
        P("dp", None),
        P(("dp", "bucket"), None),
        P(),
        P(),
        P(),
        P(),
        P(),
        P(),
    )
    return jax.shard_map(
        local,
        mesh=mesh,
        in_specs=placed,
        out_specs=(
            P(("dp", "bucket"), None),
            P(("dp", "bucket"), None),
            P("bucket", None),
            P("bucket", None),
            P("bucket", None),
            P("bucket"),
            P(),
            P(),
        ),
        check_vma=False,
    )
```
